1024 devices in a mesh: ctx: 64 (over z, x), head: 16 (over y, core).
Axes of the slice: x: 4, y: 8, z: 16, core: 2. Of those that a mesh axis runs over, the one named last changes fastest.
Arguments:
- head_input: float32 [16384, 4096], P('ctx', 'head'), may hold values from -6 to 6
- step_size: float32 [64, 16384], P('head', 'ctx'), may hold values from 0.25 to 2
- log_decay: float32 [64, 16384], P('head', 'ctx'), may hold values from -1.6 to 0
- write_proj: float32 [16384, 128], P('ctx'), may hold values from -0.375 to 0.375
- read_proj: float32 [16384, 128], P('ctx'), may hold values from -0.5 to 0.5
- grad_out: float32 [16384, 4096], P('ctx', 'head'), may hold values from -6 to 6
Outputs:
- head_output: float32 [16384, 4096], P('ctx', 'head')
- grad_input: float32 [16384, 4096], P('ctx', 'head')
- grad_step: float32 [64, 16384], P('head', 'ctx')
- write_grad: float32 [16384, 128], P(('ctx', 'head'))
- read_grad: float32 [16384, 128], P(('ctx', 'head'))
The draws below stay inside these ranges and needn't reach their ends.
All inputs are finite; a program needn't handle non-finite values.
Results may differ from the reference program's by a relative error of at most 0.00022.
Values sent between devices are 32-bit elements; how exact they have to be, the bound alone decides.
No kernel may reach another device: no remote copies, remote signals or barrier semaphores. Data moves between devices by JAX's collectives and lax.ppermute only.
A program may use at most 32 MiB of HBM per device.

```python
import math
import jax
import jax.numpy as jnp
from jax import lax

HEAD_DIM = 64
STATE = 128
GROUP = 128
TOK_DEV = 256
HEADS = 64
SEQUENCE_TOKENS = 16384


def draw_log_decay(key, part):
    random_keys = jax.random.split(key, 7)
    fast_share = 0.5
    chosen = jax.random.uniform(random_keys[0], (HEADS, 1), dtype=jnp.float32)
    fast_rate = 1.0 / 40.0 * jnp.exp(jax.random.uniform(random_keys[1], (HEADS, 1), dtype=jnp.float32, minval=-0.29, maxval=0.29))
    slow_rate = 0.25 / SEQUENCE_TOKENS * jnp.exp(jax.random.uniform(random_keys[2], (HEADS, 1), dtype=jnp.float32, minval=-0.69, maxval=0.69))
    selected_rate = jnp.where(chosen < fast_share, fast_rate, slow_rate)
    jaggedness = jnp.exp(jax.random.uniform(random_keys[3], (HEADS, SEQUENCE_TOKENS), dtype=jnp.float32, minval=-0.69, maxval=0.69))
    block_count = SEQUENCE_TOKENS // TOK_DEV
    block_multiplier = jnp.exp(jax.random.uniform(random_keys[4], (HEADS, block_count, 1), dtype=jnp.float32, minval=-0.69, maxval=0.69))
    block_multiplier = jnp.broadcast_to(block_multiplier, (HEADS, block_count, TOK_DEV)).reshape(HEADS, SEQUENCE_TOKENS)
    spike_positions = jax.random.randint(random_keys[5], (3,), 0, SEQUENCE_TOKENS)
    spike_depth = jax.random.uniform(random_keys[6], (3,), dtype=jnp.float32, minval=0.22, maxval=0.69)
    spike_locations = (jnp.arange(SEQUENCE_TOKENS)[None, :] == spike_positions[:, None]).astype(jnp.float32)
    spike_count = jnp.sum(spike_locations * spike_depth[:, None], axis=0)
    return -(selected_rate * jaggedness * block_multiplier) - spike_count[None, :]


def levels(rng, extent, cuts, smallest, largest):
    def one(axis_at, shards_of):
        heights = jax.random.uniform(jax.random.fold_in(jax.random.fold_in(rng, 6), axis_at), (shards_of,), jnp.float32, smallest / len(cuts), largest / len(cuts))
        return jnp.repeat(jnp.exp(heights), extent[axis_at] // shards_of).reshape((-1,) + (1,) * (len(extent) - axis_at - 1))

    gain = one(*cuts[0])
    for cut in cuts[1:]:
        gain = gain * one(*cut)
    return gain


def centred(key, extent, width, reach, shards=(), kind=jnp.bfloat16):
    result = jax.random.normal(key, extent, jnp.float32) * width
    if len(shards) > 0:
        result = levels(key, extent, shards, -0.22, 0.18) * result
    return jnp.clip(result, min=-reach, max=reach).astype(kind)


def setup_inputs(seed: int = 0) -> dict:
    arg_keys = jax.random.split(jax.random.key(seed), 7)
    head_input = centred(arg_keys[0], (SEQUENCE_TOKENS, HEADS * HEAD_DIM), 1.0, 6.0, ((0, 64), (1, 16)), jnp.float32)
    step_size = jnp.clip(jnp.exp(math.log(2.0) - 2.0794415 * jax.random.uniform(arg_keys[1], (HEADS, SEQUENCE_TOKENS), jnp.float32) ** levels(arg_keys[1], (HEADS, SEQUENCE_TOKENS), ((0, 16), (1, 64)), -0.2, 0.2)), 0.25, 2.0)
    log_decay = draw_log_decay(jax.random.fold_in(arg_keys[6], 71), 0)
    write_proj = centred(arg_keys[3], (SEQUENCE_TOKENS, STATE), ((SEQUENCE_TOKENS // 64) ** -0.5), 0.375, ((0, 64),), jnp.float32)
    read_proj = centred(arg_keys[4], (SEQUENCE_TOKENS, STATE), STATE ** -0.5, 0.5, ((0, 64),), jnp.float32)
    grad_out = centred(arg_keys[5], (SEQUENCE_TOKENS, HEADS * HEAD_DIM), 1.0, 6.0, ((0, 64), (1, 16)), jnp.float32)
    return dict(head_input=head_input, step_size=step_size, log_decay=log_decay, write_proj=write_proj, read_proj=read_proj, grad_out=grad_out)


def group_step(carry_state, piece):
    scaled_part, rate_part, write_part, read_part = piece
    highest = lax.Precision.HIGHEST
    cumulated = jnp.cumsum(rate_part, axis=1)
    lower_mask = jnp.tril(jnp.ones((GROUP, GROUP), dtype=bool))
    gap_logs = cumulated[:, :, None] - cumulated[:, None, :]
    decay_mat = jnp.where(lower_mask[None], jnp.exp(jnp.where(lower_mask[None], gap_logs, 0.0)), 0.0)
    inner_prod = jnp.dot(read_part, write_part.T, precision=highest)
    local_term = jnp.einsum('hts,shp->thp', inner_prod[None] * decay_mat, scaled_part, precision=highest)
    carried_term = jnp.einsum('tn,hnp->thp', read_part, carry_state, precision=highest)
    result_rows = local_term + jnp.exp(cumulated).T[:, :, None] * carried_term
    final_cum = cumulated[:, -1:]
    weighted = jnp.exp(final_cum - cumulated).T[:, :, None] * scaled_part
    update_term = jnp.einsum('sn,shp->hnp', write_part, weighted, precision=highest)
    new_state = jnp.exp(final_cum)[:, :, None] * carry_state + update_term
    return (new_state, result_rows)

def forward(head_input, step_size, write_proj, read_proj, log_decay):
    num_groups = SEQUENCE_TOKENS // GROUP
    scaled = head_input.reshape(SEQUENCE_TOKENS, HEADS, HEAD_DIM) * step_size.T[:, :, None]
    scaled = scaled.reshape(num_groups, GROUP, HEADS, HEAD_DIM)
    group_rates = log_decay.reshape(HEADS, num_groups, GROUP).transpose(1, 0, 2)
    write_parts = write_proj.reshape(num_groups, GROUP, STATE)
    read_parts = read_proj.reshape(num_groups, GROUP, STATE)
    zero_state = jnp.zeros((HEADS, STATE, HEAD_DIM), dtype=jnp.float32)
    final_state, group_results = lax.scan(jax.checkpoint(group_step), zero_state, (scaled, group_rates, write_parts, read_parts))
    return group_results.reshape(SEQUENCE_TOKENS, HEADS * HEAD_DIM)

def reference(head_input, step_size, log_decay, write_proj, read_proj, grad_out):

    def applied(input_val, step_val, write_val, read_val):
        return forward(input_val, step_val, write_val, read_val, log_decay)
    head_output, pullback = jax.vjp(applied, head_input, step_size, write_proj, read_proj)
    grad_input, grad_step, write_grad, read_grad = pullback(grad_out)
    return (head_output, grad_input, grad_step, write_grad, read_grad)
```

```python
import jax
import jax.numpy as jnp
from jax import lax
from jax.sharding import PartitionSpec as P

GROUP = 128


def prefix(x, axis, combine, identity, reverse):
    size, here = (lax.axis_size(axis), lax.axis_index(axis))
    decay, state = x
    unit = jnp.ones_like(decay)
    kept_decay, kept_state = (unit, jnp.zeros_like(state))
    shift = 1
    while shift < size:
        if reverse:
            pairs = [(j, j - shift) for j in range(shift, size)]
            reached = here < size - shift
        else:
            pairs = [(j, j + shift) for j in range(size - shift)]
            reached = here >= shift
        packed = jnp.concatenate(
            [state, jnp.broadcast_to(decay[:, None, None], state.shape[:1] + (1,) + state.shape[2:])],
            axis=1,
        )
        got = lax.ppermute(packed, axis, pairs)
        got_decay = jnp.where(reached, got[:, -1, 0], unit)
        got_state = got[:, :-1]
        kept_decay, kept_state = combine((got_decay, got_state), (kept_decay, kept_state))
        if shift * 2 < size:
            decay, state = combine((got_decay, got_state), (decay, state))
        shift *= 2
    return (kept_decay, kept_state)


def combine_forward(first_part, second_part):
    return (
        first_part[0] * second_part[0],
        second_part[1] + second_part[0][:, None, None] * first_part[1],
    )


def combine_backward(first_part, second_part):
    return (
        first_part[0] * second_part[0],
        second_part[1] + second_part[0][:, None, None] * first_part[1],
    )


def shards(head_input, step_size, log_decay, write_proj, read_proj, grad_out):
    highest = lax.Precision.HIGHEST
    head_count = step_size.shape[0]
    row_count = head_input.shape[0]
    head_width = head_input.shape[1] // head_count
    state_width = write_proj.shape[1]
    group_count = row_count // GROUP
    inputs = head_input.reshape(row_count, head_count, head_width).transpose(1, 2, 0)
    scaled = inputs * step_size[:, None, :]
    upstream = grad_out.reshape(row_count, head_count, head_width).transpose(1, 2, 0)
    row_ids = lax.broadcasted_iota(jnp.int32, (GROUP, GROUP), 0)
    col_ids = lax.broadcasted_iota(jnp.int32, (GROUP, GROUP), 1)
    lower_mask = row_ids >= col_ids
    lower_ones = lower_mask.astype(jnp.float32)
    blocks = []
    for position in range(group_count):
        offset = position * GROUP
        group_rates = log_decay[:, offset : offset + GROUP]
        scaled_part = scaled[:, :, offset : offset + GROUP]
        upstream_part = upstream[:, :, offset : offset + GROUP]
        write_part = write_proj[offset : offset + GROUP]
        read_part = read_proj[offset : offset + GROUP]
        cumulated = jnp.dot(group_rates, lower_ones.T, precision=highest)
        final_cum = cumulated[:, -1:]
        gap_logs = cumulated[:, :, None] - cumulated[:, None, :]
        decay_mat = jnp.where(
            lower_mask[None], jnp.exp(jnp.where(lower_mask[None], gap_logs, 0.0)), 0.0
        )
        inner_prod = jnp.dot(read_part, write_part.T, precision=highest)
        mixed_mat = inner_prod[None] * decay_mat
        out_near = jnp.einsum("hts,hps->hpt", mixed_mat, scaled_part, precision=highest)
        back_near = jnp.einsum("hst,hps->hpt", mixed_mat, upstream_part, precision=highest)
        pair_prods = jnp.einsum("hpt,hps->hts", upstream_part, scaled_part, precision=highest)
        weight_sum = jnp.sum(decay_mat * pair_prods, axis=0)
        read_near = jnp.dot(weight_sum, write_part, precision=highest)
        write_near = jnp.dot(weight_sum.T, read_part, precision=highest)
        into_factor = jnp.exp(cumulated)[:, None, :]
        outof_factor = jnp.exp(final_cum - cumulated)[:, None, :]
        whole_decay = jnp.exp(final_cum[:, 0])
        into_upstream = into_factor * upstream_part
        outof_scaled = outof_factor * scaled_part
        fwd_part = jnp.einsum("hps,sn->hpn", outof_scaled, write_part, precision=highest)
        bwd_part = jnp.einsum("hps,sn->hpn", into_upstream, read_part, precision=highest)
        blocks.append(
            (
                into_upstream,
                outof_scaled,
                write_part,
                read_part,
                into_factor,
                outof_factor,
                whole_decay,
                out_near,
                back_near,
                write_near,
                read_near,
                fwd_part,
                bwd_part,
            )
        )
    unit_decay = jnp.ones((head_count,), dtype=jnp.float32)
    zero_state = jnp.zeros((head_count, head_width, state_width), dtype=jnp.float32)
    fwd_decay, fwd_state = (unit_decay, zero_state)
    for entry in blocks:
        fwd_decay = fwd_decay * entry[6]
        fwd_state = entry[6][:, None, None] * fwd_state + entry[11]
    bwd_decay, bwd_state = (unit_decay, zero_state)
    for entry in reversed(blocks):
        bwd_decay = bwd_decay * entry[6]
        bwd_state = entry[12] + entry[6][:, None, None] * bwd_state
    state_in = prefix(
        (fwd_decay, fwd_state), "ctx", combine_forward, (unit_decay, zero_state), False
    )[1]
    grad_in = prefix(
        (bwd_decay, bwd_state), "ctx", combine_backward, (unit_decay, zero_state), True
    )[1]
    entering = []
    current = state_in
    for entry in blocks:
        entering.append(current)
        current = entry[6][:, None, None] * current + entry[11]
    leaving = [None] * group_count
    current = grad_in
    for position in range(group_count - 1, -1, -1):
        leaving[position] = current
        current = blocks[position][12] + blocks[position][6][:, None, None] * current
    out_blocks, back_blocks, write_far, read_far = ([], [], [], [])
    for position in range(group_count):
        into_upstream, outof_scaled, write_part, read_part, into_factor, outof_factor = blocks[
            position
        ][:6]
        state_here = entering[position]
        state_after = leaving[position]
        out_blocks.append(
            blocks[position][7]
            + into_factor * jnp.einsum("tn,hpn->hpt", read_part, state_here, precision=highest)
        )
        back_blocks.append(
            blocks[position][8]
            + outof_factor * jnp.einsum("tn,hpn->hpt", write_part, state_after, precision=highest)
        )
        read_far.append(jnp.einsum("hpt,hpn->tn", into_upstream, state_here, precision=highest))
        write_far.append(jnp.einsum("hpt,hpn->tn", outof_scaled, state_after, precision=highest))
    result_rows = jnp.concatenate(out_blocks, axis=2)
    back_rows = jnp.concatenate(back_blocks, axis=2)
    write_carried = jnp.concatenate(write_far, axis=0)
    read_carried = jnp.concatenate(read_far, axis=0)
    write_total = jnp.concatenate([entry[9] for entry in blocks], axis=0) + write_carried
    read_total = jnp.concatenate([entry[10] for entry in blocks], axis=0) + read_carried
    both_grads = lax.psum_scatter(
        jnp.concatenate([write_total, read_total], axis=1), "head", scatter_dimension=0, tiled=True
    )
    write_grad, read_grad = (both_grads[:, :state_width], both_grads[:, state_width:])
    grad_input = (
        (step_size[:, None, :] * back_rows)
        .transpose(2, 0, 1)
        .reshape(row_count, head_count * head_width)
    )
    grad_step = jnp.sum(inputs * back_rows, axis=1)
    head_output = result_rows.transpose(2, 0, 1).reshape(row_count, head_count * head_width)
    return (head_output, grad_input, grad_step, write_grad, read_grad)


def solution(mesh):
    placed = (
        P("ctx", "head"),
        P("head", "ctx"),
        P("head", "ctx"),
        P("ctx", None),
        P("ctx", None),
        P("ctx", "head"),
    )
    return jax.shard_map(
        shards,
        mesh=mesh,
        in_specs=placed,
        out_specs=(
            P("ctx", "head"),
            P("ctx", "head"),
            P("head", "ctx"),
            P(("ctx", "head"), None),
            P(("ctx", "head"), None),
        ),
        check_vma=False,
    )
```

```python
import jax
import jax.numpy as jnp
from jax import lax
from jax.sharding import PartitionSpec as P

GROUP = 128


def both_prefixes(decay, fwd_state, bwd_state, axis):
    size, here = (lax.axis_size(axis), lax.axis_index(axis))
    unit = jnp.ones_like(decay)
    zero = jnp.zeros_like(fwd_state)
    before_decay, before_state = (unit, zero)
    after_decay, after_state = (unit, zero)
    span_decay, span_fwd, span_bwd = (decay, fwd_state, bwd_state)
    extra = decay.shape[:1] + (1,) + fwd_state.shape[2:]
    shift = 1
    while shift < size:
        pairs = [(j, j ^ shift) for j in range(size)]
        packed = jnp.concatenate(
            [span_fwd, span_bwd, jnp.broadcast_to(span_decay[:, None, None], extra)], axis=1
        )
        got = lax.ppermute(packed, axis, pairs)
        width = fwd_state.shape[1]
        got_fwd, got_bwd, got_decay = (got[:, :width], got[:, width : 2 * width], got[:, -1, 0])
        upper = (here & shift) != 0
        scale = before_decay[:, None, None]
        before_state = jnp.where(upper, before_state + scale * got_fwd, before_state)
        before_decay = jnp.where(upper, before_decay * got_decay, before_decay)
        scale = after_decay[:, None, None]
        after_state = jnp.where(upper, after_state, after_state + scale * got_bwd)
        after_decay = jnp.where(upper, after_decay, after_decay * got_decay)
        if shift * 2 < size:
            mine = span_decay[:, None, None]
            theirs = got_decay[:, None, None]
            span_fwd = jnp.where(upper, span_fwd + mine * got_fwd, got_fwd + theirs * span_fwd)
            span_bwd = jnp.where(upper, got_bwd + theirs * span_bwd, span_bwd + mine * got_bwd)
            span_decay = span_decay * got_decay
        shift *= 2
    return (before_state, after_state)


def halving_scatter(total, axis):
    size, here = (lax.axis_size(axis), lax.axis_index(axis))
    rows = total.shape[0] // size
    bits = size.bit_length() - 1
    work = total.reshape((2,) * bits + (rows,) + total.shape[1:])
    for bit in range(bits):
        shift = 1 << bit
        upper = (here & shift) != 0
        place = bits - 1 - bit
        low = lax.index_in_dim(work, 0, place, keepdims=False)
        high = lax.index_in_dim(work, 1, place, keepdims=False)
        keep = jnp.where(upper, high, low)
        send = jnp.where(upper, low, high)
        got = lax.ppermute(send, axis, [(j, j ^ shift) for j in range(size)])
        work = keep + got
    return work


def combine_forward(first_part, second_part):
    return (
        first_part[0] * second_part[0],
        second_part[1] + second_part[0][:, None, None] * first_part[1],
    )


def combine_backward(first_part, second_part):
    return (
        first_part[0] * second_part[0],
        second_part[1] + second_part[0][:, None, None] * first_part[1],
    )


def shards(head_input, step_size, log_decay, write_proj, read_proj, grad_out):
    highest = lax.Precision.HIGHEST
    head_count = step_size.shape[0]
    row_count = head_input.shape[0]
    head_width = head_input.shape[1] // head_count
    state_width = write_proj.shape[1]
    group_count = row_count // GROUP
    inputs = head_input.reshape(row_count, head_count, head_width).transpose(1, 2, 0)
    scaled = inputs * step_size[:, None, :]
    upstream = grad_out.reshape(row_count, head_count, head_width).transpose(1, 2, 0)
    row_ids = lax.broadcasted_iota(jnp.int32, (GROUP, GROUP), 0)
    col_ids = lax.broadcasted_iota(jnp.int32, (GROUP, GROUP), 1)
    lower_mask = row_ids >= col_ids
    lower_ones = lower_mask.astype(jnp.float32)
    blocks = []
    for position in range(group_count):
        offset = position * GROUP
        group_rates = log_decay[:, offset : offset + GROUP]
        scaled_part = scaled[:, :, offset : offset + GROUP]
        upstream_part = upstream[:, :, offset : offset + GROUP]
        write_part = write_proj[offset : offset + GROUP]
        read_part = read_proj[offset : offset + GROUP]
        cumulated = jnp.dot(group_rates, lower_ones.T, precision=highest)
        final_cum = cumulated[:, -1:]
        gap_logs = cumulated[:, :, None] - cumulated[:, None, :]
        decay_mat = jnp.where(
            lower_mask[None], jnp.exp(jnp.where(lower_mask[None], gap_logs, 0.0)), 0.0
        )
        inner_prod = jnp.dot(read_part, write_part.T, precision=highest)
        mixed_mat = inner_prod[None] * decay_mat
        out_near = jnp.einsum("hts,hps->hpt", mixed_mat, scaled_part, precision=highest)
        back_near = jnp.einsum("hst,hps->hpt", mixed_mat, upstream_part, precision=highest)
        pair_prods = jnp.einsum("hpt,hps->hts", upstream_part, scaled_part, precision=highest)
        weight_sum = jnp.sum(decay_mat * pair_prods, axis=0)
        read_near = jnp.dot(weight_sum, write_part, precision=highest)
        write_near = jnp.dot(weight_sum.T, read_part, precision=highest)
        into_factor = jnp.exp(cumulated)[:, None, :]
        outof_factor = jnp.exp(final_cum - cumulated)[:, None, :]
        whole_decay = jnp.exp(final_cum[:, 0])
        into_upstream = into_factor * upstream_part
        outof_scaled = outof_factor * scaled_part
        fwd_part = jnp.einsum("hps,sn->hpn", outof_scaled, write_part, precision=highest)
        bwd_part = jnp.einsum("hps,sn->hpn", into_upstream, read_part, precision=highest)
        blocks.append(
            (
                into_upstream,
                outof_scaled,
                write_part,
                read_part,
                into_factor,
                outof_factor,
                whole_decay,
                out_near,
                back_near,
                write_near,
                read_near,
                fwd_part,
                bwd_part,
            )
        )
    unit_decay = jnp.ones((head_count,), dtype=jnp.float32)
    zero_state = jnp.zeros((head_count, head_width, state_width), dtype=jnp.float32)
    fwd_decay, fwd_state = (unit_decay, zero_state)
    for entry in blocks:
        fwd_decay = fwd_decay * entry[6]
        fwd_state = entry[6][:, None, None] * fwd_state + entry[11]
    bwd_decay, bwd_state = (unit_decay, zero_state)
    for entry in reversed(blocks):
        bwd_decay = bwd_decay * entry[6]
        bwd_state = entry[12] + entry[6][:, None, None] * bwd_state
    state_in, grad_in = both_prefixes(fwd_decay, fwd_state, bwd_state, "ctx")
    entering = []
    current = state_in
    for entry in blocks:
        entering.append(current)
        current = entry[6][:, None, None] * current + entry[11]
    leaving = [None] * group_count
    current = grad_in
    for position in range(group_count - 1, -1, -1):
        leaving[position] = current
        current = blocks[position][12] + blocks[position][6][:, None, None] * current
    out_blocks, back_blocks, write_far, read_far = ([], [], [], [])
    for position in range(group_count):
        into_upstream, outof_scaled, write_part, read_part, into_factor, outof_factor = blocks[
            position
        ][:6]
        state_here = entering[position]
        state_after = leaving[position]
        out_blocks.append(
            blocks[position][7]
            + into_factor * jnp.einsum("tn,hpn->hpt", read_part, state_here, precision=highest)
        )
        back_blocks.append(
            blocks[position][8]
            + outof_factor * jnp.einsum("tn,hpn->hpt", write_part, state_after, precision=highest)
        )
        read_far.append(jnp.einsum("hpt,hpn->tn", into_upstream, state_here, precision=highest))
        write_far.append(jnp.einsum("hpt,hpn->tn", outof_scaled, state_after, precision=highest))
    result_rows = jnp.concatenate(out_blocks, axis=2)
    back_rows = jnp.concatenate(back_blocks, axis=2)
    write_carried = jnp.concatenate(write_far, axis=0)
    read_carried = jnp.concatenate(read_far, axis=0)
    write_total = jnp.concatenate([entry[9] for entry in blocks], axis=0) + write_carried
    read_total = jnp.concatenate([entry[10] for entry in blocks], axis=0) + read_carried
    both_grads = halving_scatter(jnp.concatenate([write_total, read_total], axis=1), "head")
    write_grad, read_grad = (both_grads[:, :state_width], both_grads[:, state_width:])
    grad_input = (
        (step_size[:, None, :] * back_rows)
        .transpose(2, 0, 1)
        .reshape(row_count, head_count * head_width)
    )
    grad_step = jnp.sum(inputs * back_rows, axis=1)
    head_output = result_rows.transpose(2, 0, 1).reshape(row_count, head_count * head_width)
    return (head_output, grad_input, grad_step, write_grad, read_grad)


def solution(mesh):
    placed = (
        P("ctx", "head"),
        P("head", "ctx"),
        P("head", "ctx"),
        P("ctx", None),
        P("ctx", None),
        P("ctx", "head"),
    )
    return jax.shard_map(
        shards,
        mesh=mesh,
        in_specs=placed,
        out_specs=(
            P("ctx", "head"),
            P("ctx", "head"),
            P("head", "ctx"),
            P(("ctx", "head"), None),
            P(("ctx", "head"), None),
        ),
        check_vma=False,
    )
```

```python
import jax
import jax.numpy as jnp
from jax import lax
from jax.sharding import PartitionSpec as P

GROUP = 128


def butterfly_rounds(shifts, size, here, span, before, after, final):
    span_decay, span_fwd, span_bwd = span
    before_decay, before_state = before
    after_decay, after_state = after
    width = span_fwd.shape[1]
    extra = span_decay.shape[:1] + (1,) + span_fwd.shape[2:]
    for at, shift in enumerate(shifts):
        last = final and at == len(shifts) - 1
        upper = (here & shift) != 0
        pairs = [(j, j ^ shift) for j in range(size)]
        tail = jnp.broadcast_to(span_decay[:, None, None], extra)
        if last:
            packed = jnp.concatenate([jnp.where(upper, span_bwd, span_fwd), tail], axis=1)
        else:
            packed = jnp.concatenate([span_fwd, span_bwd, tail], axis=1)
        got = lax.ppermute(packed, "ctx", pairs)
        got_decay = got[:, -1, 0]
        if last:
            got_fwd = got_bwd = got[:, :width]
        else:
            got_fwd, got_bwd = (got[:, :width], got[:, width : 2 * width])
        scale = before_decay[:, None, None]
        before_state = jnp.where(upper, before_state + scale * got_fwd, before_state)
        before_decay = jnp.where(upper, before_decay * got_decay, before_decay)
        scale = after_decay[:, None, None]
        after_state = jnp.where(upper, after_state, after_state + scale * got_bwd)
        after_decay = jnp.where(upper, after_decay, after_decay * got_decay)
        if not last:
            mine = span_decay[:, None, None]
            theirs = got_decay[:, None, None]
            span_fwd = jnp.where(upper, span_fwd + mine * got_fwd, got_fwd + theirs * span_fwd)
            span_bwd = jnp.where(upper, got_bwd + theirs * span_bwd, span_bwd + mine * got_bwd)
            span_decay = span_decay * got_decay
    return ((span_decay, span_fwd, span_bwd), (before_decay, before_state), (after_decay, after_state))


def both_prefixes(decay, fwd_state, bwd_state, axis):
    size, here = (lax.axis_size(axis), lax.axis_index(axis))
    heads = decay.shape[0]
    unit = jnp.ones_like(decay)
    zero = jnp.zeros_like(fwd_state)
    inner = 1
    while inner < heads and inner < size:
        inner *= 2
    inner_shifts = []
    shift = 1
    while shift < inner:
        inner_shifts.append(shift)
        shift *= 2
    outer_shifts = []
    while shift < size:
        outer_shifts.append(shift)
        shift *= 2
    span, before, after = butterfly_rounds(
        inner_shifts, size, here, (decay, fwd_state, bwd_state), (unit, zero), (unit, zero), False
    )
    part = heads // inner
    slot = here % inner
    span = jax.tree.map(lambda a: lax.dynamic_slice_in_dim(a, slot * part, part, axis=0), span)
    unit_part = jnp.ones_like(span[0])
    zero_part = jnp.zeros_like(span[1])
    _, outer_before, outer_after = butterfly_rounds(
        outer_shifts, size, here, span, (unit_part, zero_part), (unit_part, zero_part), True
    )
    shared = jnp.concatenate([outer_before[1], outer_after[1]], axis=1)
    for shift in inner_shifts:
        upper = (here & shift) != 0
        got = lax.ppermute(shared, axis, [(j, j ^ shift) for j in range(size)])
        shared = jnp.where(
            upper, jnp.concatenate([got, shared], axis=0), jnp.concatenate([shared, got], axis=0)
        )
    width = fwd_state.shape[1]
    state_in = before[1] + before[0][:, None, None] * shared[:, :width]
    grad_in = after[1] + after[0][:, None, None] * shared[:, width:]
    return (state_in, grad_in)


def halving_scatter(total, axis):
    size, here = (lax.axis_size(axis), lax.axis_index(axis))
    rows = total.shape[0] // size
    bits = size.bit_length() - 1
    work = total.reshape((2,) * bits + (rows,) + total.shape[1:])
    for bit in range(bits):
        shift = 1 << bit
        upper = (here & shift) != 0
        place = bits - 1 - bit
        low = lax.index_in_dim(work, 0, place, keepdims=False)
        high = lax.index_in_dim(work, 1, place, keepdims=False)
        keep = jnp.where(upper, high, low)
        send = jnp.where(upper, low, high)
        got = lax.ppermute(send, axis, [(j, j ^ shift) for j in range(size)])
        work = keep + got
    return work


def combine_forward(first_part, second_part):
    return (
        first_part[0] * second_part[0],
        second_part[1] + second_part[0][:, None, None] * first_part[1],
    )


def combine_backward(first_part, second_part):
    return (
        first_part[0] * second_part[0],
        second_part[1] + second_part[0][:, None, None] * first_part[1],
    )


def shards(head_input, step_size, log_decay, write_proj, read_proj, grad_out):
    highest = lax.Precision.HIGHEST
    head_count = step_size.shape[0]
    row_count = head_input.shape[0]
    head_width = head_input.shape[1] // head_count
    state_width = write_proj.shape[1]
    group_count = row_count // GROUP
    inputs = head_input.reshape(row_count, head_count, head_width).transpose(1, 2, 0)
    scaled = inputs * step_size[:, None, :]
    upstream = grad_out.reshape(row_count, head_count, head_width).transpose(1, 2, 0)
    row_ids = lax.broadcasted_iota(jnp.int32, (GROUP, GROUP), 0)
    col_ids = lax.broadcasted_iota(jnp.int32, (GROUP, GROUP), 1)
    lower_mask = row_ids >= col_ids
    lower_ones = lower_mask.astype(jnp.float32)
    blocks = []
    for position in range(group_count):
        offset = position * GROUP
        group_rates = log_decay[:, offset : offset + GROUP]
        scaled_part = scaled[:, :, offset : offset + GROUP]
        upstream_part = upstream[:, :, offset : offset + GROUP]
        write_part = write_proj[offset : offset + GROUP]
        read_part = read_proj[offset : offset + GROUP]
        cumulated = jnp.dot(group_rates, lower_ones.T, precision=highest)
        final_cum = cumulated[:, -1:]
        gap_logs = cumulated[:, :, None] - cumulated[:, None, :]
        decay_mat = jnp.where(
            lower_mask[None], jnp.exp(jnp.where(lower_mask[None], gap_logs, 0.0)), 0.0
        )
        inner_prod = jnp.dot(read_part, write_part.T, precision=highest)
        mixed_mat = inner_prod[None] * decay_mat
        out_near = jnp.einsum("hts,hps->hpt", mixed_mat, scaled_part, precision=highest)
        back_near = jnp.einsum("hst,hps->hpt", mixed_mat, upstream_part, precision=highest)
        pair_prods = jnp.einsum("hpt,hps->hts", upstream_part, scaled_part, precision=highest)
        weight_sum = jnp.sum(decay_mat * pair_prods, axis=0)
        read_near = jnp.dot(weight_sum, write_part, precision=highest)
        write_near = jnp.dot(weight_sum.T, read_part, precision=highest)
        into_factor = jnp.exp(cumulated)[:, None, :]
        outof_factor = jnp.exp(final_cum - cumulated)[:, None, :]
        whole_decay = jnp.exp(final_cum[:, 0])
        into_upstream = into_factor * upstream_part
        outof_scaled = outof_factor * scaled_part
        fwd_part = jnp.einsum("hps,sn->hpn", outof_scaled, write_part, precision=highest)
        bwd_part = jnp.einsum("hps,sn->hpn", into_upstream, read_part, precision=highest)
        blocks.append(
            (
                into_upstream,
                outof_scaled,
                write_part,
                read_part,
                into_factor,
                outof_factor,
                whole_decay,
                out_near,
                back_near,
                write_near,
                read_near,
                fwd_part,
                bwd_part,
            )
        )
    unit_decay = jnp.ones((head_count,), dtype=jnp.float32)
    zero_state = jnp.zeros((head_count, head_width, state_width), dtype=jnp.float32)
    fwd_decay, fwd_state = (unit_decay, zero_state)
    for entry in blocks:
        fwd_decay = fwd_decay * entry[6]
        fwd_state = entry[6][:, None, None] * fwd_state + entry[11]
    bwd_decay, bwd_state = (unit_decay, zero_state)
    for entry in reversed(blocks):
        bwd_decay = bwd_decay * entry[6]
        bwd_state = entry[12] + entry[6][:, None, None] * bwd_state
    state_in, grad_in = both_prefixes(fwd_decay, fwd_state, bwd_state, "ctx")
    entering = []
    current = state_in
    for entry in blocks:
        entering.append(current)
        current = entry[6][:, None, None] * current + entry[11]
    leaving = [None] * group_count
    current = grad_in
    for position in range(group_count - 1, -1, -1):
        leaving[position] = current
        current = blocks[position][12] + blocks[position][6][:, None, None] * current
    out_blocks, back_blocks, write_far, read_far = ([], [], [], [])
    for position in range(group_count):
        into_upstream, outof_scaled, write_part, read_part, into_factor, outof_factor = blocks[
            position
        ][:6]
        state_here = entering[position]
        state_after = leaving[position]
        out_blocks.append(
            blocks[position][7]
            + into_factor * jnp.einsum("tn,hpn->hpt", read_part, state_here, precision=highest)
        )
        back_blocks.append(
            blocks[position][8]
            + outof_factor * jnp.einsum("tn,hpn->hpt", write_part, state_after, precision=highest)
        )
        read_far.append(jnp.einsum("hpt,hpn->tn", into_upstream, state_here, precision=highest))
        write_far.append(jnp.einsum("hpt,hpn->tn", outof_scaled, state_after, precision=highest))
    result_rows = jnp.concatenate(out_blocks, axis=2)
    back_rows = jnp.concatenate(back_blocks, axis=2)
    write_carried = jnp.concatenate(write_far, axis=0)
    read_carried = jnp.concatenate(read_far, axis=0)
    write_total = jnp.concatenate([entry[9] for entry in blocks], axis=0) + write_carried
    read_total = jnp.concatenate([entry[10] for entry in blocks], axis=0) + read_carried
    both_grads = halving_scatter(jnp.concatenate([write_total, read_total], axis=1), "head")
    write_grad, read_grad = (both_grads[:, :state_width], both_grads[:, state_width:])
    grad_input = (
        (step_size[:, None, :] * back_rows)
        .transpose(2, 0, 1)
        .reshape(row_count, head_count * head_width)
    )
    grad_step = jnp.sum(inputs * back_rows, axis=1)
    head_output = result_rows.transpose(2, 0, 1).reshape(row_count, head_count * head_width)
    return (head_output, grad_input, grad_step, write_grad, read_grad)


def solution(mesh):
    placed = (
        P("ctx", "head"),
        P("head", "ctx"),
        P("head", "ctx"),
        P("ctx", None),
        P("ctx", None),
        P("ctx", "head"),
    )
    return jax.shard_map(
        shards,
        mesh=mesh,
        in_specs=placed,
        out_specs=(
            P("ctx", "head"),
            P("ctx", "head"),
            P("head", "ctx"),
            P(("ctx", "head"), None),
            P(("ctx", "head"), None),
        ),
        check_vma=False,
    )
```

```python
import jax
import jax.numpy as jnp
from jax import lax
from jax.sharding import Mesh, PartitionSpec as P

GROUP = 128


def butterfly_rounds(shifts, size, here, span, before, after, final, axis):
    span_decay, span_fwd, span_bwd = span
    before_decay, before_state = before
    after_decay, after_state = after
    width = span_fwd.shape[1]
    extra = span_decay.shape[:1] + (1,) + span_fwd.shape[2:]
    for at, shift in enumerate(shifts):
        last = final and at == len(shifts) - 1
        upper = (here & shift) != 0
        pairs = [(j, j ^ shift) for j in range(size)]
        tail = jnp.broadcast_to(span_decay[:, None, None], extra)
        if last:
            packed = jnp.concatenate([jnp.where(upper, span_bwd, span_fwd), tail], axis=1)
        else:
            packed = jnp.concatenate([span_fwd, span_bwd, tail], axis=1)
        got = lax.ppermute(packed, axis, pairs)
        got_decay = got[:, -1, 0]
        if last:
            got_fwd = got_bwd = got[:, :width]
        else:
            got_fwd, got_bwd = (got[:, :width], got[:, width : 2 * width])
        scale = before_decay[:, None, None]
        before_state = jnp.where(upper, before_state + scale * got_fwd, before_state)
        before_decay = jnp.where(upper, before_decay * got_decay, before_decay)
        scale = after_decay[:, None, None]
        after_state = jnp.where(upper, after_state, after_state + scale * got_bwd)
        after_decay = jnp.where(upper, after_decay, after_decay * got_decay)
        if not last:
            mine = span_decay[:, None, None]
            theirs = got_decay[:, None, None]
            span_fwd = jnp.where(upper, span_fwd + mine * got_fwd, got_fwd + theirs * span_fwd)
            span_bwd = jnp.where(upper, got_bwd + theirs * span_bwd, span_bwd + mine * got_bwd)
            span_decay = span_decay * got_decay
    return ((span_decay, span_fwd, span_bwd), (before_decay, before_state), (after_decay, after_state))


def both_prefixes(decay, fwd_state, bwd_state):
    outer_size, here = (lax.axis_size("outer"), lax.axis_index("outer"))
    members = lax.axis_size("inner")
    width = fwd_state.shape[1]
    packed = jnp.concatenate(
        [fwd_state, bwd_state, jnp.broadcast_to(decay[:, None, None], decay.shape[:1] + (1,) + fwd_state.shape[2:])],
        axis=1,
    )
    mine = lax.all_to_all(packed, "inner", 0, 0, tiled=True)
    part = mine.shape[0] // members
    rows = mine.reshape((members, part) + mine.shape[1:])
    fwd_rows, bwd_rows, decay_rows = (rows[:, :, :width], rows[:, :, width : 2 * width], rows[:, :, -1, 0])
    unit = jnp.ones_like(decay_rows[0])
    zero = jnp.zeros_like(fwd_rows[0])
    run_decay, run_state = (unit, zero)
    before_decays, before_states = ([], [])
    for m in range(members):
        before_decays.append(run_decay)
        before_states.append(run_state)
        run_state = decay_rows[m][:, None, None] * run_state + fwd_rows[m]
        run_decay = run_decay * decay_rows[m]
    group = (run_decay, run_state)
    run_decay, run_state = (unit, zero)
    after_decays, after_states = ([None] * members, [None] * members)
    for m in range(members - 1, -1, -1):
        after_decays[m] = run_decay
        after_states[m] = run_state
        run_state = bwd_rows[m] + decay_rows[m][:, None, None] * run_state
        run_decay = run_decay * decay_rows[m]
    shifts = []
    shift = 1
    while shift < outer_size:
        shifts.append(shift)
        shift *= 2
    _, outer_before, outer_after = butterfly_rounds(
        shifts, outer_size, here, (group[0], group[1], run_state), (unit, zero), (unit, zero), True, "outer"
    )
    back = jnp.stack(
        [
            jnp.concatenate(
                [
                    before_states[m] + before_decays[m][:, None, None] * outer_before[1],
                    after_states[m] + after_decays[m][:, None, None] * outer_after[1],
                ],
                axis=1,
            )
            for m in range(members)
        ]
    )
    shared = lax.all_to_all(back.reshape((members * part,) + back.shape[2:]), "inner", 0, 0, tiled=True)
    return (shared[:, :width], shared[:, width:])


def head_scatter(total, axis):
    size = lax.axis_size(axis)
    pieces = total.reshape((size, total.shape[0] // size) + total.shape[1:])
    return jnp.sum(lax.all_to_all(pieces, axis, 0, 0), axis=0)


def combine_forward(first_part, second_part):
    return (
        first_part[0] * second_part[0],
        second_part[1] + second_part[0][:, None, None] * first_part[1],
    )


def combine_backward(first_part, second_part):
    return (
        first_part[0] * second_part[0],
        second_part[1] + second_part[0][:, None, None] * first_part[1],
    )


def shards(head_input, step_size, log_decay, write_proj, read_proj, grad_out):
    highest = lax.Precision.HIGHEST
    head_count = step_size.shape[0]
    row_count = head_input.shape[0]
    head_width = head_input.shape[1] // head_count
    state_width = write_proj.shape[1]
    group_count = row_count // GROUP
    inputs = head_input.reshape(row_count, head_count, head_width).transpose(1, 2, 0)
    scaled = inputs * step_size[:, None, :]
    upstream = grad_out.reshape(row_count, head_count, head_width).transpose(1, 2, 0)
    row_ids = lax.broadcasted_iota(jnp.int32, (GROUP, GROUP), 0)
    col_ids = lax.broadcasted_iota(jnp.int32, (GROUP, GROUP), 1)
    lower_mask = row_ids >= col_ids
    lower_ones = lower_mask.astype(jnp.float32)
    blocks = []
    for position in range(group_count):
        offset = position * GROUP
        group_rates = log_decay[:, offset : offset + GROUP]
        scaled_part = scaled[:, :, offset : offset + GROUP]
        upstream_part = upstream[:, :, offset : offset + GROUP]
        write_part = write_proj[offset : offset + GROUP]
        read_part = read_proj[offset : offset + GROUP]
        cumulated = jnp.dot(group_rates, lower_ones.T, precision=highest)
        final_cum = cumulated[:, -1:]
        gap_logs = cumulated[:, :, None] - cumulated[:, None, :]
        decay_mat = jnp.where(
            lower_mask[None], jnp.exp(jnp.where(lower_mask[None], gap_logs, 0.0)), 0.0
        )
        inner_prod = jnp.dot(read_part, write_part.T, precision=highest)
        mixed_mat = inner_prod[None] * decay_mat
        out_near = jnp.einsum("hts,hps->hpt", mixed_mat, scaled_part, precision=highest)
        back_near = jnp.einsum("hst,hps->hpt", mixed_mat, upstream_part, precision=highest)
        pair_prods = jnp.einsum("hpt,hps->hts", upstream_part, scaled_part, precision=highest)
        weight_sum = jnp.sum(decay_mat * pair_prods, axis=0)
        read_near = jnp.dot(weight_sum, write_part, precision=highest)
        write_near = jnp.dot(weight_sum.T, read_part, precision=highest)
        into_factor = jnp.exp(cumulated)[:, None, :]
        outof_factor = jnp.exp(final_cum - cumulated)[:, None, :]
        whole_decay = jnp.exp(final_cum[:, 0])
        into_upstream = into_factor * upstream_part
        outof_scaled = outof_factor * scaled_part
        fwd_part = jnp.einsum("hps,sn->hpn", outof_scaled, write_part, precision=highest)
        bwd_part = jnp.einsum("hps,sn->hpn", into_upstream, read_part, precision=highest)
        blocks.append(
            (
                into_upstream,
                outof_scaled,
                write_part,
                read_part,
                into_factor,
                outof_factor,
                whole_decay,
                out_near,
                back_near,
                write_near,
                read_near,
                fwd_part,
                bwd_part,
            )
        )
    unit_decay = jnp.ones((head_count,), dtype=jnp.float32)
    zero_state = jnp.zeros((head_count, head_width, state_width), dtype=jnp.float32)
    fwd_decay, fwd_state = (unit_decay, zero_state)
    for entry in blocks:
        fwd_decay = fwd_decay * entry[6]
        fwd_state = entry[6][:, None, None] * fwd_state + entry[11]
    bwd_decay, bwd_state = (unit_decay, zero_state)
    for entry in reversed(blocks):
        bwd_decay = bwd_decay * entry[6]
        bwd_state = entry[12] + entry[6][:, None, None] * bwd_state
    state_in, grad_in = both_prefixes(fwd_decay, fwd_state, bwd_state)
    entering = []
    current = state_in
    for entry in blocks:
        entering.append(current)
        current = entry[6][:, None, None] * current + entry[11]
    leaving = [None] * group_count
    current = grad_in
    for position in range(group_count - 1, -1, -1):
        leaving[position] = current
        current = blocks[position][12] + blocks[position][6][:, None, None] * current
    out_blocks, back_blocks, write_far, read_far = ([], [], [], [])
    for position in range(group_count):
        into_upstream, outof_scaled, write_part, read_part, into_factor, outof_factor = blocks[
            position
        ][:6]
        state_here = entering[position]
        state_after = leaving[position]
        out_blocks.append(
            blocks[position][7]
            + into_factor * jnp.einsum("tn,hpn->hpt", read_part, state_here, precision=highest)
        )
        back_blocks.append(
            blocks[position][8]
            + outof_factor * jnp.einsum("tn,hpn->hpt", write_part, state_after, precision=highest)
        )
        read_far.append(jnp.einsum("hpt,hpn->tn", into_upstream, state_here, precision=highest))
        write_far.append(jnp.einsum("hpt,hpn->tn", outof_scaled, state_after, precision=highest))
    result_rows = jnp.concatenate(out_blocks, axis=2)
    back_rows = jnp.concatenate(back_blocks, axis=2)
    write_carried = jnp.concatenate(write_far, axis=0)
    read_carried = jnp.concatenate(read_far, axis=0)
    write_total = jnp.concatenate([entry[9] for entry in blocks], axis=0) + write_carried
    read_total = jnp.concatenate([entry[10] for entry in blocks], axis=0) + read_carried
    both_grads = head_scatter(jnp.concatenate([write_total, read_total], axis=1), "head")
    write_grad, read_grad = (both_grads[:, :state_width], both_grads[:, state_width:])
    grad_input = (
        (step_size[:, None, :] * back_rows)
        .transpose(2, 0, 1)
        .reshape(row_count, head_count * head_width)
    )
    grad_step = jnp.sum(inputs * back_rows, axis=1)
    head_output = result_rows.transpose(2, 0, 1).reshape(row_count, head_count * head_width)
    return (head_output, grad_input, grad_step, write_grad, read_grad)


def solution(mesh):
    def run(*args):
        heads_here = args[1].shape[0] // mesh.shape["head"]
        ctx_count = mesh.shape["ctx"]
        inner = 1
        while inner < heads_here and inner < ctx_count and heads_here % (inner * 2) == 0:
            inner *= 2
        fine = Mesh(
            mesh.devices.reshape((ctx_count // inner, inner) + mesh.devices.shape[1:]),
            ("outer", "inner", "head"),
        )
        ctx = ("outer", "inner")
        placed = (
            P(ctx, "head"),
            P("head", ctx),
            P("head", ctx),
            P(ctx, None),
            P(ctx, None),
            P(ctx, "head"),
        )
        return jax.shard_map(
            shards,
            mesh=fine,
            in_specs=placed,
            out_specs=(
                P(ctx, "head"),
                P(ctx, "head"),
                P("head", ctx),
                P(ctx + ("head",), None),
                P(ctx + ("head",), None),
            ),
            check_vma=False,
        )(*args)

    return run
```

```python
import functools

import jax
import jax.numpy as jnp
from jax import lax
from jax.sharding import Mesh, PartitionSpec as P

GROUP = 128


def butterfly_rounds(shifts, size, here, span, before, after, final, axis):
    span_decay, span_fwd, span_bwd = span
    before_decay, before_state = before
    after_decay, after_state = after
    width = span_fwd.shape[1]
    extra = span_decay.shape[:1] + (1,) + span_fwd.shape[2:]
    for at, shift in enumerate(shifts):
        last = final and at == len(shifts) - 1
        upper = (here & shift) != 0
        pairs = [(j, j ^ shift) for j in range(size)]
        tail = jnp.broadcast_to(span_decay[:, None, None], extra)
        if last:
            packed = jnp.concatenate([jnp.where(upper, span_bwd, span_fwd), tail], axis=1)
        else:
            packed = jnp.concatenate([span_fwd, span_bwd, tail], axis=1)
        got = lax.ppermute(packed, axis, pairs)
        got_decay = got[:, -1, 0]
        if last:
            got_fwd = got_bwd = got[:, :width]
        else:
            got_fwd, got_bwd = (got[:, :width], got[:, width : 2 * width])
        scale = before_decay[:, None, None]
        before_state = jnp.where(upper, before_state + scale * got_fwd, before_state)
        before_decay = jnp.where(upper, before_decay * got_decay, before_decay)
        scale = after_decay[:, None, None]
        after_state = jnp.where(upper, after_state, after_state + scale * got_bwd)
        after_decay = jnp.where(upper, after_decay, after_decay * got_decay)
        if not last:
            mine = span_decay[:, None, None]
            theirs = got_decay[:, None, None]
            span_fwd = jnp.where(upper, span_fwd + mine * got_fwd, got_fwd + theirs * span_fwd)
            span_bwd = jnp.where(upper, got_bwd + theirs * span_bwd, span_bwd + mine * got_bwd)
            span_decay = span_decay * got_decay
    return ((span_decay, span_fwd, span_bwd), (before_decay, before_state), (after_decay, after_state))


def level_exchange(aggregate, axis, last):
    count, here = (lax.axis_size(axis), lax.axis_index(axis))
    decay, fwd, bwd = aggregate
    width = fwd.shape[1]
    tail = jnp.broadcast_to(decay[:, None, None], decay.shape[:1] + (1,) + fwd.shape[2:])
    if last:
        sent = jnp.stack(
            [jnp.concatenate([jnp.where(m < here, bwd, fwd), tail], axis=1) for m in range(count)]
        )
    else:
        packed = jnp.concatenate([fwd, bwd, tail], axis=1)
        sent = jnp.broadcast_to(packed[None], (count,) + packed.shape)
    got = lax.all_to_all(sent, axis, 0, 0)
    got_decay = got[:, :, -1, 0]
    got_fwd = got[:, :, :width]
    got_bwd = got_fwd if last else got[:, :, width : 2 * width]
    unit = jnp.ones_like(decay)
    zero = jnp.zeros_like(fwd)
    before_decay, before_state = (unit, zero)
    for s in range(count):
        take = s < here
        before_state = jnp.where(take, got_decay[s][:, None, None] * before_state + got_fwd[s], before_state)
        before_decay = jnp.where(take, before_decay * got_decay[s], before_decay)
    after_decay, after_state = (unit, zero)
    for s in range(count - 1, -1, -1):
        take = s > here
        after_state = jnp.where(take, got_bwd[s] + got_decay[s][:, None, None] * after_state, after_state)
        after_decay = jnp.where(take, after_decay * got_decay[s], after_decay)
    if last:
        return ((before_decay, before_state), (after_decay, after_state), None)
    span_decay, span_fwd, span_bwd = (unit, zero, zero)
    for s in range(count):
        span_fwd = got_decay[s][:, None, None] * span_fwd + got_fwd[s]
        span_decay = span_decay * got_decay[s]
    for s in range(count - 1, -1, -1):
        span_bwd = got_bwd[s] + got_decay[s][:, None, None] * span_bwd
    return ((before_decay, before_state), (after_decay, after_state), (span_decay, span_fwd, span_bwd))


def both_prefixes(decay, fwd_state, bwd_state, levels):
    members = lax.axis_size("inner")
    width = fwd_state.shape[1]
    packed = jnp.concatenate(
        [fwd_state, bwd_state, jnp.broadcast_to(decay[:, None, None], decay.shape[:1] + (1,) + fwd_state.shape[2:])],
        axis=1,
    )
    mine = lax.all_to_all(packed, "inner", 0, 0, tiled=True)
    part = mine.shape[0] // members
    rows = mine.reshape((members, part) + mine.shape[1:])
    fwd_rows, bwd_rows, decay_rows = (rows[:, :, :width], rows[:, :, width : 2 * width], rows[:, :, -1, 0])
    unit = jnp.ones_like(decay_rows[0])
    zero = jnp.zeros_like(fwd_rows[0])
    run_decay, run_state = (unit, zero)
    before_decays, before_states = ([], [])
    for m in range(members):
        before_decays.append(run_decay)
        before_states.append(run_state)
        run_state = decay_rows[m][:, None, None] * run_state + fwd_rows[m]
        run_decay = run_decay * decay_rows[m]
    aggregate = (run_decay, run_state, None)
    run_decay, run_state = (unit, zero)
    after_decays, after_states = ([None] * members, [None] * members)
    for m in range(members - 1, -1, -1):
        after_decays[m] = run_decay
        after_states[m] = run_state
        run_state = bwd_rows[m] + decay_rows[m][:, None, None] * run_state
        run_decay = run_decay * decay_rows[m]
    aggregate = (aggregate[0], aggregate[1], run_state)
    total_before = (unit, zero)
    total_after = (unit, zero)
    for at, axis in enumerate(levels):
        before, after, aggregate = level_exchange(aggregate, axis, at == len(levels) - 1)
        total_before = (before[0] * total_before[0], total_before[1] + total_before[0][:, None, None] * before[1])
        total_after = (after[0] * total_after[0], total_after[1] + total_after[0][:, None, None] * after[1])
    back = jnp.stack(
        [
            jnp.concatenate(
                [
                    before_states[m] + before_decays[m][:, None, None] * total_before[1],
                    after_states[m] + after_decays[m][:, None, None] * total_after[1],
                ],
                axis=1,
            )
            for m in range(members)
        ]
    )
    shared = lax.all_to_all(back.reshape((members * part,) + back.shape[2:]), "inner", 0, 0, tiled=True)
    return (shared[:, :width], shared[:, width:])


def head_scatter(total, axis):
    size = lax.axis_size(axis)
    pieces = total.reshape((size, total.shape[0] // size) + total.shape[1:])
    return jnp.sum(lax.all_to_all(pieces, axis, 0, 0), axis=0)


def combine_forward(first_part, second_part):
    return (
        first_part[0] * second_part[0],
        second_part[1] + second_part[0][:, None, None] * first_part[1],
    )


def combine_backward(first_part, second_part):
    return (
        first_part[0] * second_part[0],
        second_part[1] + second_part[0][:, None, None] * first_part[1],
    )


def shards(head_input, step_size, log_decay, write_proj, read_proj, grad_out, levels):
    highest = lax.Precision.HIGHEST
    head_count = step_size.shape[0]
    row_count = head_input.shape[0]
    head_width = head_input.shape[1] // head_count
    state_width = write_proj.shape[1]
    group_count = row_count // GROUP
    inputs = head_input.reshape(row_count, head_count, head_width).transpose(1, 2, 0)
    scaled = inputs * step_size[:, None, :]
    upstream = grad_out.reshape(row_count, head_count, head_width).transpose(1, 2, 0)
    row_ids = lax.broadcasted_iota(jnp.int32, (GROUP, GROUP), 0)
    col_ids = lax.broadcasted_iota(jnp.int32, (GROUP, GROUP), 1)
    lower_mask = row_ids >= col_ids
    lower_ones = lower_mask.astype(jnp.float32)
    blocks = []
    for position in range(group_count):
        offset = position * GROUP
        group_rates = log_decay[:, offset : offset + GROUP]
        scaled_part = scaled[:, :, offset : offset + GROUP]
        upstream_part = upstream[:, :, offset : offset + GROUP]
        write_part = write_proj[offset : offset + GROUP]
        read_part = read_proj[offset : offset + GROUP]
        cumulated = jnp.dot(group_rates, lower_ones.T, precision=highest)
        final_cum = cumulated[:, -1:]
        gap_logs = cumulated[:, :, None] - cumulated[:, None, :]
        decay_mat = jnp.where(
            lower_mask[None], jnp.exp(jnp.where(lower_mask[None], gap_logs, 0.0)), 0.0
        )
        inner_prod = jnp.dot(read_part, write_part.T, precision=highest)
        mixed_mat = inner_prod[None] * decay_mat
        out_near = jnp.einsum("hts,hps->hpt", mixed_mat, scaled_part, precision=highest)
        back_near = jnp.einsum("hst,hps->hpt", mixed_mat, upstream_part, precision=highest)
        pair_prods = jnp.einsum("hpt,hps->hts", upstream_part, scaled_part, precision=highest)
        weight_sum = jnp.sum(decay_mat * pair_prods, axis=0)
        read_near = jnp.dot(weight_sum, write_part, precision=highest)
        write_near = jnp.dot(weight_sum.T, read_part, precision=highest)
        into_factor = jnp.exp(cumulated)[:, None, :]
        outof_factor = jnp.exp(final_cum - cumulated)[:, None, :]
        whole_decay = jnp.exp(final_cum[:, 0])
        into_upstream = into_factor * upstream_part
        outof_scaled = outof_factor * scaled_part
        fwd_part = jnp.einsum("hps,sn->hpn", outof_scaled, write_part, precision=highest)
        bwd_part = jnp.einsum("hps,sn->hpn", into_upstream, read_part, precision=highest)
        blocks.append(
            (
                into_upstream,
                outof_scaled,
                write_part,
                read_part,
                into_factor,
                outof_factor,
                whole_decay,
                out_near,
                back_near,
                write_near,
                read_near,
                fwd_part,
                bwd_part,
            )
        )
    unit_decay = jnp.ones((head_count,), dtype=jnp.float32)
    zero_state = jnp.zeros((head_count, head_width, state_width), dtype=jnp.float32)
    fwd_decay, fwd_state = (unit_decay, zero_state)
    for entry in blocks:
        fwd_decay = fwd_decay * entry[6]
        fwd_state = entry[6][:, None, None] * fwd_state + entry[11]
    bwd_decay, bwd_state = (unit_decay, zero_state)
    for entry in reversed(blocks):
        bwd_decay = bwd_decay * entry[6]
        bwd_state = entry[12] + entry[6][:, None, None] * bwd_state
    state_in, grad_in = both_prefixes(fwd_decay, fwd_state, bwd_state, levels)
    entering = []
    current = state_in
    for entry in blocks:
        entering.append(current)
        current = entry[6][:, None, None] * current + entry[11]
    leaving = [None] * group_count
    current = grad_in
    for position in range(group_count - 1, -1, -1):
        leaving[position] = current
        current = blocks[position][12] + blocks[position][6][:, None, None] * current
    out_blocks, back_blocks, write_far, read_far = ([], [], [], [])
    for position in range(group_count):
        into_upstream, outof_scaled, write_part, read_part, into_factor, outof_factor = blocks[
            position
        ][:6]
        state_here = entering[position]
        state_after = leaving[position]
        out_blocks.append(
            blocks[position][7]
            + into_factor * jnp.einsum("tn,hpn->hpt", read_part, state_here, precision=highest)
        )
        back_blocks.append(
            blocks[position][8]
            + outof_factor * jnp.einsum("tn,hpn->hpt", write_part, state_after, precision=highest)
        )
        read_far.append(jnp.einsum("hpt,hpn->tn", into_upstream, state_here, precision=highest))
        write_far.append(jnp.einsum("hpt,hpn->tn", outof_scaled, state_after, precision=highest))
    result_rows = jnp.concatenate(out_blocks, axis=2)
    back_rows = jnp.concatenate(back_blocks, axis=2)
    write_carried = jnp.concatenate(write_far, axis=0)
    read_carried = jnp.concatenate(read_far, axis=0)
    write_total = jnp.concatenate([entry[9] for entry in blocks], axis=0) + write_carried
    read_total = jnp.concatenate([entry[10] for entry in blocks], axis=0) + read_carried
    both_grads = head_scatter(jnp.concatenate([write_total, read_total], axis=1), "head")
    write_grad, read_grad = (both_grads[:, :state_width], both_grads[:, state_width:])
    grad_input = (
        (step_size[:, None, :] * back_rows)
        .transpose(2, 0, 1)
        .reshape(row_count, head_count * head_width)
    )
    grad_step = jnp.sum(inputs * back_rows, axis=1)
    head_output = result_rows.transpose(2, 0, 1).reshape(row_count, head_count * head_width)
    return (head_output, grad_input, grad_step, write_grad, read_grad)


def solution(mesh):
    def run(*args):
        heads_here = args[1].shape[0] // mesh.shape["head"]
        ctx_count = mesh.shape["ctx"]
        inner = 1
        while inner < heads_here and inner < ctx_count and heads_here % (inner * 2) == 0:
            inner *= 2
        rest = ctx_count // inner
        factors = []
        while rest > 1:
            factor = 4 if rest % 4 == 0 else (2 if rest % 2 == 0 else rest)
            factors.append(factor)
            rest //= factor
        levels = tuple(f"level{k}" for k in range(len(factors)))
        fine = Mesh(
            mesh.devices.reshape(tuple(reversed(factors)) + (inner,) + mesh.devices.shape[1:]),
            tuple(reversed(levels)) + ("inner", "head"),
        )
        ctx = tuple(reversed(levels)) + ("inner",)
        placed = (
            P(ctx, "head"),
            P("head", ctx),
            P("head", ctx),
            P(ctx, None),
            P(ctx, None),
            P(ctx, "head"),
        )
        return jax.shard_map(
            functools.partial(shards, levels=levels),
            mesh=fine,
            in_specs=placed,
            out_specs=(
                P(ctx, "head"),
                P(ctx, "head"),
                P("head", ctx),
                P(ctx + ("head",), None),
                P(ctx + ("head",), None),
            ),
            check_vma=False,
        )(*args)

    return run
```

```python
import functools

import jax
import jax.numpy as jnp
from jax import lax
from jax.experimental import pallas as pl
from jax.experimental.pallas import tpu as pltpu
from jax.sharding import Mesh, PartitionSpec as P

GROUP = 128


def butterfly_rounds(shifts, size, here, span, before, after, final, axis):
    span_decay, span_fwd, span_bwd = span
    before_decay, before_state = before
    after_decay, after_state = after
    width = span_fwd.shape[1]
    extra = span_decay.shape[:1] + (1,) + span_fwd.shape[2:]
    for at, shift in enumerate(shifts):
        last = final and at == len(shifts) - 1
        upper = (here & shift) != 0
        pairs = [(j, j ^ shift) for j in range(size)]
        tail = jnp.broadcast_to(span_decay[:, None, None], extra)
        if last:
            packed = jnp.concatenate([jnp.where(upper, span_bwd, span_fwd), tail], axis=1)
        else:
            packed = jnp.concatenate([span_fwd, span_bwd, tail], axis=1)
        got = lax.ppermute(packed, axis, pairs)
        got_decay = got[:, -1, 0]
        if last:
            got_fwd = got_bwd = got[:, :width]
        else:
            got_fwd, got_bwd = (got[:, :width], got[:, width : 2 * width])
        scale = before_decay[:, None, None]
        before_state = jnp.where(upper, before_state + scale * got_fwd, before_state)
        before_decay = jnp.where(upper, before_decay * got_decay, before_decay)
        scale = after_decay[:, None, None]
        after_state = jnp.where(upper, after_state, after_state + scale * got_bwd)
        after_decay = jnp.where(upper, after_decay, after_decay * got_decay)
        if not last:
            mine = span_decay[:, None, None]
            theirs = got_decay[:, None, None]
            span_fwd = jnp.where(upper, span_fwd + mine * got_fwd, got_fwd + theirs * span_fwd)
            span_bwd = jnp.where(upper, got_bwd + theirs * span_bwd, span_bwd + mine * got_bwd)
            span_decay = span_decay * got_decay
    return ((span_decay, span_fwd, span_bwd), (before_decay, before_state), (after_decay, after_state))


INTERPRET = False


def level_kernel(count, width, last):
    rows = width + 1 if last else 2 * width + 1

    def kernel(here_ref, got_ref, *outs):
        here = here_ref[0]
        decays = [got_ref[s, rows - 1 : rows, :] for s in range(count)]
        fwds = [got_ref[s, 0:width, :] for s in range(count)]
        bwds = fwds if last else [got_ref[s, width : 2 * width, :] for s in range(count)]
        before_state = jnp.zeros((width, 128), jnp.float32)
        before_decay = jnp.ones((1, 128), jnp.float32)
        for s in range(count):
            take = s < here
            factor = jnp.where(take, decays[s], 1.0)
            before_state = factor * before_state + jnp.where(take, fwds[s], 0.0)
            before_decay = before_decay * factor
        after_state = jnp.zeros((width, 128), jnp.float32)
        after_decay = jnp.ones((1, 128), jnp.float32)
        for s in range(count - 1, -1, -1):
            take = s > here
            factor = jnp.where(take, decays[s], 1.0)
            after_state = jnp.where(take, bwds[s], 0.0) + factor * after_state
            after_decay = after_decay * factor
        outs[0][...] = before_state
        outs[1][...] = before_decay
        outs[2][...] = after_state
        outs[3][...] = after_decay
        if not last:
            span_fwd = jnp.zeros((width, 128), jnp.float32)
            span_decay = jnp.ones((1, 128), jnp.float32)
            for s in range(count):
                span_fwd = decays[s] * span_fwd + fwds[s]
                span_decay = span_decay * decays[s]
            span_bwd = jnp.zeros((width, 128), jnp.float32)
            for s in range(count - 1, -1, -1):
                span_bwd = bwds[s] + decays[s] * span_bwd
            outs[4][...] = span_fwd
            outs[5][...] = span_bwd
            outs[6][...] = span_decay

    state = jax.ShapeDtypeStruct((width, 128), jnp.float32)
    row = jax.ShapeDtypeStruct((1, 128), jnp.float32)
    shapes = (state, row, state, row) + (() if last else (state, state, row))
    vmem = pl.BlockSpec(memory_space=pltpu.VMEM)
    return pl.pallas_call(
        kernel,
        out_shape=shapes,
        in_specs=[pl.BlockSpec(memory_space=pltpu.SMEM), vmem],
        out_specs=tuple(vmem for _ in shapes),
        interpret=INTERPRET,
    )


def level_exchange(aggregate, axis, last):
    count, here = (lax.axis_size(axis), lax.axis_index(axis))
    decay, fwd, bwd = aggregate
    width = fwd.shape[1]
    tail = jnp.broadcast_to(decay[:, None, None], decay.shape[:1] + (1,) + fwd.shape[2:])
    if last:
        sent = jnp.stack(
            [jnp.concatenate([jnp.where(m < here, bwd, fwd), tail], axis=1) for m in range(count)]
        )
    else:
        packed = jnp.concatenate([fwd, bwd, tail], axis=1)
        sent = jnp.broadcast_to(packed[None], (count,) + packed.shape)
    got = lax.all_to_all(sent, axis, 0, 0)
    got = got.reshape((count,) + got.shape[2:])
    outs = level_kernel(count, width, last)(jnp.reshape(here, (1,)).astype(jnp.int32), got)
    before = (outs[1][:, 0], outs[0][None])
    after = (outs[3][:, 0], outs[2][None])
    if last:
        return (before, after, None)
    return (before, after, (outs[6][:, 0], outs[4][None], outs[5][None]))


def both_prefixes(decay, fwd_state, bwd_state, levels):
    members = lax.axis_size("inner")
    width = fwd_state.shape[1]
    packed = jnp.concatenate(
        [fwd_state, bwd_state, jnp.broadcast_to(decay[:, None, None], decay.shape[:1] + (1,) + fwd_state.shape[2:])],
        axis=1,
    )
    mine = lax.all_to_all(packed, "inner", 0, 0, tiled=True)
    part = mine.shape[0] // members
    rows = mine.reshape((members, part) + mine.shape[1:])
    fwd_rows, bwd_rows, decay_rows = (rows[:, :, :width], rows[:, :, width : 2 * width], rows[:, :, -1, 0])
    unit = jnp.ones_like(decay_rows[0])
    zero = jnp.zeros_like(fwd_rows[0])
    run_decay, run_state = (unit, zero)
    before_decays, before_states = ([], [])
    for m in range(members):
        before_decays.append(run_decay)
        before_states.append(run_state)
        run_state = decay_rows[m][:, None, None] * run_state + fwd_rows[m]
        run_decay = run_decay * decay_rows[m]
    aggregate = (run_decay, run_state, None)
    run_decay, run_state = (unit, zero)
    after_decays, after_states = ([None] * members, [None] * members)
    for m in range(members - 1, -1, -1):
        after_decays[m] = run_decay
        after_states[m] = run_state
        run_state = bwd_rows[m] + decay_rows[m][:, None, None] * run_state
        run_decay = run_decay * decay_rows[m]
    aggregate = (aggregate[0], aggregate[1], run_state)
    total_before = (unit, zero)
    total_after = (unit, zero)
    for at, axis in enumerate(levels):
        before, after, aggregate = level_exchange(aggregate, axis, at == len(levels) - 1)
        total_before = (before[0] * total_before[0], total_before[1] + total_before[0][:, None, None] * before[1])
        total_after = (after[0] * total_after[0], total_after[1] + total_after[0][:, None, None] * after[1])
    back = jnp.stack(
        [
            jnp.concatenate(
                [
                    before_states[m] + before_decays[m][:, None, None] * total_before[1],
                    after_states[m] + after_decays[m][:, None, None] * total_after[1],
                ],
                axis=1,
            )
            for m in range(members)
        ]
    )
    shared = lax.all_to_all(back.reshape((members * part,) + back.shape[2:]), "inner", 0, 0, tiled=True)
    return (shared[:, :width], shared[:, width:])


def head_scatter(total, axis):
    size = lax.axis_size(axis)
    pieces = total.reshape((size, total.shape[0] // size) + total.shape[1:])
    return jnp.sum(lax.all_to_all(pieces, axis, 0, 0), axis=0)


def combine_forward(first_part, second_part):
    return (
        first_part[0] * second_part[0],
        second_part[1] + second_part[0][:, None, None] * first_part[1],
    )


def combine_backward(first_part, second_part):
    return (
        first_part[0] * second_part[0],
        second_part[1] + second_part[0][:, None, None] * first_part[1],
    )


def shards(head_input, step_size, log_decay, write_proj, read_proj, grad_out, levels):
    highest = lax.Precision.HIGHEST
    head_count = step_size.shape[0]
    row_count = head_input.shape[0]
    head_width = head_input.shape[1] // head_count
    state_width = write_proj.shape[1]
    group_count = row_count // GROUP
    inputs = head_input.reshape(row_count, head_count, head_width).transpose(1, 2, 0)
    scaled = inputs * step_size[:, None, :]
    upstream = grad_out.reshape(row_count, head_count, head_width).transpose(1, 2, 0)
    row_ids = lax.broadcasted_iota(jnp.int32, (GROUP, GROUP), 0)
    col_ids = lax.broadcasted_iota(jnp.int32, (GROUP, GROUP), 1)
    lower_mask = row_ids >= col_ids
    lower_ones = lower_mask.astype(jnp.float32)
    blocks = []
    for position in range(group_count):
        offset = position * GROUP
        group_rates = log_decay[:, offset : offset + GROUP]
        scaled_part = scaled[:, :, offset : offset + GROUP]
        upstream_part = upstream[:, :, offset : offset + GROUP]
        write_part = write_proj[offset : offset + GROUP]
        read_part = read_proj[offset : offset + GROUP]
        cumulated = jnp.dot(group_rates, lower_ones.T, precision=highest)
        final_cum = cumulated[:, -1:]
        gap_logs = cumulated[:, :, None] - cumulated[:, None, :]
        decay_mat = jnp.where(
            lower_mask[None], jnp.exp(jnp.where(lower_mask[None], gap_logs, 0.0)), 0.0
        )
        inner_prod = jnp.dot(read_part, write_part.T, precision=highest)
        mixed_mat = inner_prod[None] * decay_mat
        out_near = jnp.einsum("hts,hps->hpt", mixed_mat, scaled_part, precision=highest)
        back_near = jnp.einsum("hst,hps->hpt", mixed_mat, upstream_part, precision=highest)
        pair_prods = jnp.einsum("hpt,hps->hts", upstream_part, scaled_part, precision=highest)
        weight_sum = jnp.sum(decay_mat * pair_prods, axis=0)
        read_near = jnp.dot(weight_sum, write_part, precision=highest)
        write_near = jnp.dot(weight_sum.T, read_part, precision=highest)
        into_factor = jnp.exp(cumulated)[:, None, :]
        outof_factor = jnp.exp(final_cum - cumulated)[:, None, :]
        whole_decay = jnp.exp(final_cum[:, 0])
        into_upstream = into_factor * upstream_part
        outof_scaled = outof_factor * scaled_part
        fwd_part = jnp.einsum("hps,sn->hpn", outof_scaled, write_part, precision=highest)
        bwd_part = jnp.einsum("hps,sn->hpn", into_upstream, read_part, precision=highest)
        blocks.append(
            (
                into_upstream,
                outof_scaled,
                write_part,
                read_part,
                into_factor,
                outof_factor,
                whole_decay,
                out_near,
                back_near,
                write_near,
                read_near,
                fwd_part,
                bwd_part,
            )
        )
    unit_decay = jnp.ones((head_count,), dtype=jnp.float32)
    zero_state = jnp.zeros((head_count, head_width, state_width), dtype=jnp.float32)
    fwd_decay, fwd_state = (unit_decay, zero_state)
    for entry in blocks:
        fwd_decay = fwd_decay * entry[6]
        fwd_state = entry[6][:, None, None] * fwd_state + entry[11]
    bwd_decay, bwd_state = (unit_decay, zero_state)
    for entry in reversed(blocks):
        bwd_decay = bwd_decay * entry[6]
        bwd_state = entry[12] + entry[6][:, None, None] * bwd_state
    state_in, grad_in = both_prefixes(fwd_decay, fwd_state, bwd_state, levels)
    entering = []
    current = state_in
    for entry in blocks:
        entering.append(current)
        current = entry[6][:, None, None] * current + entry[11]
    leaving = [None] * group_count
    current = grad_in
    for position in range(group_count - 1, -1, -1):
        leaving[position] = current
        current = blocks[position][12] + blocks[position][6][:, None, None] * current
    out_blocks, back_blocks, write_far, read_far = ([], [], [], [])
    for position in range(group_count):
        into_upstream, outof_scaled, write_part, read_part, into_factor, outof_factor = blocks[
            position
        ][:6]
        state_here = entering[position]
        state_after = leaving[position]
        out_blocks.append(
            blocks[position][7]
            + into_factor * jnp.einsum("tn,hpn->hpt", read_part, state_here, precision=highest)
        )
        back_blocks.append(
            blocks[position][8]
            + outof_factor * jnp.einsum("tn,hpn->hpt", write_part, state_after, precision=highest)
        )
        read_far.append(jnp.einsum("hpt,hpn->tn", into_upstream, state_here, precision=highest))
        write_far.append(jnp.einsum("hpt,hpn->tn", outof_scaled, state_after, precision=highest))
    result_rows = jnp.concatenate(out_blocks, axis=2)
    back_rows = jnp.concatenate(back_blocks, axis=2)
    write_carried = jnp.concatenate(write_far, axis=0)
    read_carried = jnp.concatenate(read_far, axis=0)
    write_total = jnp.concatenate([entry[9] for entry in blocks], axis=0) + write_carried
    read_total = jnp.concatenate([entry[10] for entry in blocks], axis=0) + read_carried
    both_grads = head_scatter(jnp.concatenate([write_total, read_total], axis=1), "head")
    write_grad, read_grad = (both_grads[:, :state_width], both_grads[:, state_width:])
    grad_input = (
        (step_size[:, None, :] * back_rows)
        .transpose(2, 0, 1)
        .reshape(row_count, head_count * head_width)
    )
    grad_step = jnp.sum(inputs * back_rows, axis=1)
    head_output = result_rows.transpose(2, 0, 1).reshape(row_count, head_count * head_width)
    return (head_output, grad_input, grad_step, write_grad, read_grad)


def solution(mesh):
    def run(*args):
        heads_here = args[1].shape[0] // mesh.shape["head"]
        ctx_count = mesh.shape["ctx"]
        inner = 1
        while inner < heads_here and inner < ctx_count and heads_here % (inner * 2) == 0:
            inner *= 2
        rest = ctx_count // inner
        factors = []
        while rest > 1:
            factor = 4 if rest % 4 == 0 else (2 if rest % 2 == 0 else rest)
            factors.append(factor)
            rest //= factor
        levels = tuple(f"level{k}" for k in range(len(factors)))
        fine = Mesh(
            mesh.devices.reshape(tuple(reversed(factors)) + (inner,) + mesh.devices.shape[1:]),
            tuple(reversed(levels)) + ("inner", "head"),
        )
        ctx = tuple(reversed(levels)) + ("inner",)
        placed = (
            P(ctx, "head"),
            P("head", ctx),
            P("head", ctx),
            P(ctx, None),
            P(ctx, None),
            P(ctx, "head"),
        )
        return jax.shard_map(
            functools.partial(shards, levels=levels),
            mesh=fine,
            in_specs=placed,
            out_specs=(
                P(ctx, "head"),
                P(ctx, "head"),
                P("head", ctx),
                P(ctx + ("head",), None),
                P(ctx + ("head",), None),
            ),
            check_vma=False,
        )(*args)

    return run
```

```python
import functools

import jax
import jax.numpy as jnp
from jax import lax
from jax.experimental import pallas as pl
from jax.experimental.pallas import tpu as pltpu
from jax.sharding import Mesh, PartitionSpec as P

GROUP = 128


def butterfly_rounds(shifts, size, here, span, before, after, final, axis):
    span_decay, span_fwd, span_bwd = span
    before_decay, before_state = before
    after_decay, after_state = after
    width = span_fwd.shape[1]
    extra = span_decay.shape[:1] + (1,) + span_fwd.shape[2:]
    for at, shift in enumerate(shifts):
        last = final and at == len(shifts) - 1
        upper = (here & shift) != 0
        pairs = [(j, j ^ shift) for j in range(size)]
        tail = jnp.broadcast_to(span_decay[:, None, None], extra)
        if last:
            packed = jnp.concatenate([jnp.where(upper, span_bwd, span_fwd), tail], axis=1)
        else:
            packed = jnp.concatenate([span_fwd, span_bwd, tail], axis=1)
        got = lax.ppermute(packed, axis, pairs)
        got_decay = got[:, -1, 0]
        if last:
            got_fwd = got_bwd = got[:, :width]
        else:
            got_fwd, got_bwd = (got[:, :width], got[:, width : 2 * width])
        scale = before_decay[:, None, None]
        before_state = jnp.where(upper, before_state + scale * got_fwd, before_state)
        before_decay = jnp.where(upper, before_decay * got_decay, before_decay)
        scale = after_decay[:, None, None]
        after_state = jnp.where(upper, after_state, after_state + scale * got_bwd)
        after_decay = jnp.where(upper, after_decay, after_decay * got_decay)
        if not last:
            mine = span_decay[:, None, None]
            theirs = got_decay[:, None, None]
            span_fwd = jnp.where(upper, span_fwd + mine * got_fwd, got_fwd + theirs * span_fwd)
            span_bwd = jnp.where(upper, got_bwd + theirs * span_bwd, span_bwd + mine * got_bwd)
            span_decay = span_decay * got_decay
    return ((span_decay, span_fwd, span_bwd), (before_decay, before_state), (after_decay, after_state))


INTERPRET = False


def level_kernel(count, width, last):
    rows = width + 1 if last else 2 * width + 1

    def kernel(here_ref, got_ref, *outs):
        here = here_ref[0]
        decays = [got_ref[s, rows - 1 : rows, :] for s in range(count)]
        fwds = [got_ref[s, 0:width, :] for s in range(count)]
        bwds = fwds if last else [got_ref[s, width : 2 * width, :] for s in range(count)]
        before_state = jnp.zeros((width, 128), jnp.float32)
        before_decay = jnp.ones((1, 128), jnp.float32)
        for s in range(count):
            take = s < here
            factor = jnp.where(take, decays[s], 1.0)
            before_state = factor * before_state + jnp.where(take, fwds[s], 0.0)
            before_decay = before_decay * factor
        after_state = jnp.zeros((width, 128), jnp.float32)
        after_decay = jnp.ones((1, 128), jnp.float32)
        for s in range(count - 1, -1, -1):
            take = s > here
            factor = jnp.where(take, decays[s], 1.0)
            after_state = jnp.where(take, bwds[s], 0.0) + factor * after_state
            after_decay = after_decay * factor
        outs[0][...] = before_state
        outs[1][...] = before_decay
        outs[2][...] = after_state
        outs[3][...] = after_decay
        if not last:
            span_fwd = jnp.zeros((width, 128), jnp.float32)
            span_decay = jnp.ones((1, 128), jnp.float32)
            for s in range(count):
                span_fwd = decays[s] * span_fwd + fwds[s]
                span_decay = span_decay * decays[s]
            span_bwd = jnp.zeros((width, 128), jnp.float32)
            for s in range(count - 1, -1, -1):
                span_bwd = bwds[s] + decays[s] * span_bwd
            outs[4][...] = span_fwd
            outs[5][...] = span_bwd
            outs[6][...] = span_decay

    state = jax.ShapeDtypeStruct((width, 128), jnp.float32)
    row = jax.ShapeDtypeStruct((1, 128), jnp.float32)
    shapes = (state, row, state, row) + (() if last else (state, state, row))
    vmem = pl.BlockSpec(memory_space=pltpu.VMEM)
    return pl.pallas_call(
        kernel,
        out_shape=shapes,
        in_specs=[pl.BlockSpec(memory_space=pltpu.SMEM), vmem],
        out_specs=tuple(vmem for _ in shapes),
        interpret=INTERPRET,
    )


def level_exchange(aggregate, axis, last):
    count, here = (lax.axis_size(axis), lax.axis_index(axis))
    decay, fwd, bwd = aggregate
    width = fwd.shape[1]
    tail = jnp.broadcast_to(decay[:, None, None], decay.shape[:1] + (1,) + fwd.shape[2:])
    if last:
        sent = jnp.stack(
            [jnp.concatenate([jnp.where(m < here, bwd, fwd), tail], axis=1) for m in range(count)]
        )
    else:
        packed = jnp.concatenate([fwd, bwd, tail], axis=1)
        sent = jnp.broadcast_to(packed[None], (count,) + packed.shape)
    got = lax.all_to_all(sent, axis, 0, 0)
    got = got.reshape((count,) + got.shape[2:])
    outs = level_kernel(count, width, last)(jnp.reshape(here, (1,)).astype(jnp.int32), got)
    before = (outs[1][:, 0], outs[0][None])
    after = (outs[3][:, 0], outs[2][None])
    if last:
        return (before, after, None)
    return (before, after, (outs[6][:, 0], outs[4][None], outs[5][None]))


def inner_kernel(members, width):
    def kernel(mine_ref, bs_ref, bd_ref, as_ref, ad_ref, sf_ref, sb_ref, sd_ref):
        rows = 2 * width + 1
        decays = [mine_ref[m, rows - 1 : rows, :] for m in range(members)]
        run_state = jnp.zeros((width, 128), jnp.float32)
        run_decay = jnp.ones((1, 128), jnp.float32)
        for m in range(members):
            bs_ref[m] = run_state
            bd_ref[m] = run_decay
            run_state = decays[m] * run_state + mine_ref[m, 0:width, :]
            run_decay = run_decay * decays[m]
        sf_ref[...] = run_state
        sd_ref[...] = run_decay
        run_state = jnp.zeros((width, 128), jnp.float32)
        run_decay = jnp.ones((1, 128), jnp.float32)
        for m in range(members - 1, -1, -1):
            as_ref[m] = run_state
            ad_ref[m] = run_decay
            run_state = mine_ref[m, width : 2 * width, :] + decays[m] * run_state
            run_decay = run_decay * decays[m]
        sb_ref[...] = run_state

    many = jax.ShapeDtypeStruct((members, width, 128), jnp.float32)
    many_rows = jax.ShapeDtypeStruct((members, 1, 128), jnp.float32)
    state = jax.ShapeDtypeStruct((width, 128), jnp.float32)
    row = jax.ShapeDtypeStruct((1, 128), jnp.float32)
    shapes = (many, many_rows, many, many_rows, state, state, row)
    vmem = pl.BlockSpec(memory_space=pltpu.VMEM)
    return pl.pallas_call(
        kernel, out_shape=shapes, in_specs=[vmem], out_specs=tuple(vmem for _ in shapes), interpret=INTERPRET
    )


def back_kernel(members, width, level_count):
    def kernel(*refs):
        bs_ref, bd_ref, as_ref, ad_ref = refs[:4]
        level_refs = refs[4 : 4 + 4 * level_count]
        out_ref = refs[-1]
        before_state = jnp.zeros((width, 128), jnp.float32)
        before_decay = jnp.ones((1, 128), jnp.float32)
        after_state = jnp.zeros((width, 128), jnp.float32)
        after_decay = jnp.ones((1, 128), jnp.float32)
        for k in range(level_count):
            lbs, lbd, las, lad = level_refs[4 * k : 4 * k + 4]
            before_state = before_state + before_decay * lbs[...]
            before_decay = before_decay * lbd[...]
            after_state = after_state + after_decay * las[...]
            after_decay = after_decay * lad[...]
        for m in range(members):
            out_ref[m, 0:width, :] = bs_ref[m] + bd_ref[m] * before_state
            out_ref[m, width : 2 * width, :] = as_ref[m] + ad_ref[m] * after_state

    vmem = pl.BlockSpec(memory_space=pltpu.VMEM)
    return pl.pallas_call(
        kernel,
        out_shape=jax.ShapeDtypeStruct((members, 2 * width, 128), jnp.float32),
        in_specs=[vmem] * (4 + 4 * level_count),
        out_specs=vmem,
        interpret=INTERPRET,
    )


def both_prefixes(decay, fwd_state, bwd_state, levels):
    members = lax.axis_size("inner")
    width = fwd_state.shape[1]
    packed = jnp.concatenate(
        [fwd_state, bwd_state, jnp.broadcast_to(decay[:, None, None], decay.shape[:1] + (1,) + fwd_state.shape[2:])],
        axis=1,
    )
    mine = lax.all_to_all(packed, "inner", 0, 0, tiled=True)
    prefixes = inner_kernel(members, width)(mine)
    aggregate = (prefixes[6][:, 0], prefixes[4][None], prefixes[5][None])
    level_parts = []
    for at, axis in enumerate(levels):
        before, after, aggregate = level_exchange(aggregate, axis, at == len(levels) - 1)
        level_parts += [before[1][0], jnp.broadcast_to(before[0][:, None], (1, 128)),
                        after[1][0], jnp.broadcast_to(after[0][:, None], (1, 128))]
    back = back_kernel(members, width, len(levels))(*prefixes[:4], *level_parts)
    shared = lax.all_to_all(back, "inner", 0, 0, tiled=True)
    return (shared[:, :width], shared[:, width:])


def head_scatter(total, axis):
    size = lax.axis_size(axis)
    pieces = total.reshape((size, total.shape[0] // size) + total.shape[1:])
    return jnp.sum(lax.all_to_all(pieces, axis, 0, 0), axis=0)


def combine_forward(first_part, second_part):
    return (
        first_part[0] * second_part[0],
        second_part[1] + second_part[0][:, None, None] * first_part[1],
    )


def combine_backward(first_part, second_part):
    return (
        first_part[0] * second_part[0],
        second_part[1] + second_part[0][:, None, None] * first_part[1],
    )


def shards(head_input, step_size, log_decay, write_proj, read_proj, grad_out, levels):
    highest = lax.Precision.HIGHEST
    head_count = step_size.shape[0]
    row_count = head_input.shape[0]
    head_width = head_input.shape[1] // head_count
    state_width = write_proj.shape[1]
    group_count = row_count // GROUP
    inputs = head_input.reshape(row_count, head_count, head_width).transpose(1, 2, 0)
    scaled = inputs * step_size[:, None, :]
    upstream = grad_out.reshape(row_count, head_count, head_width).transpose(1, 2, 0)
    row_ids = lax.broadcasted_iota(jnp.int32, (GROUP, GROUP), 0)
    col_ids = lax.broadcasted_iota(jnp.int32, (GROUP, GROUP), 1)
    lower_mask = row_ids >= col_ids
    lower_ones = lower_mask.astype(jnp.float32)
    blocks = []
    for position in range(group_count):
        offset = position * GROUP
        group_rates = log_decay[:, offset : offset + GROUP]
        scaled_part = scaled[:, :, offset : offset + GROUP]
        upstream_part = upstream[:, :, offset : offset + GROUP]
        write_part = write_proj[offset : offset + GROUP]
        read_part = read_proj[offset : offset + GROUP]
        cumulated = jnp.dot(group_rates, lower_ones.T, precision=highest)
        final_cum = cumulated[:, -1:]
        gap_logs = cumulated[:, :, None] - cumulated[:, None, :]
        decay_mat = jnp.where(
            lower_mask[None], jnp.exp(jnp.where(lower_mask[None], gap_logs, 0.0)), 0.0
        )
        inner_prod = jnp.dot(read_part, write_part.T, precision=highest)
        mixed_mat = inner_prod[None] * decay_mat
        out_near = jnp.einsum("hts,hps->hpt", mixed_mat, scaled_part, precision=highest)
        back_near = jnp.einsum("hst,hps->hpt", mixed_mat, upstream_part, precision=highest)
        pair_prods = jnp.einsum("hpt,hps->hts", upstream_part, scaled_part, precision=highest)
        weight_sum = jnp.sum(decay_mat * pair_prods, axis=0)
        read_near = jnp.dot(weight_sum, write_part, precision=highest)
        write_near = jnp.dot(weight_sum.T, read_part, precision=highest)
        into_factor = jnp.exp(cumulated)[:, None, :]
        outof_factor = jnp.exp(final_cum - cumulated)[:, None, :]
        whole_decay = jnp.exp(final_cum[:, 0])
        into_upstream = into_factor * upstream_part
        outof_scaled = outof_factor * scaled_part
        fwd_part = jnp.einsum("hps,sn->hpn", outof_scaled, write_part, precision=highest)
        bwd_part = jnp.einsum("hps,sn->hpn", into_upstream, read_part, precision=highest)
        blocks.append(
            (
                into_upstream,
                outof_scaled,
                write_part,
                read_part,
                into_factor,
                outof_factor,
                whole_decay,
                out_near,
                back_near,
                write_near,
                read_near,
                fwd_part,
                bwd_part,
            )
        )
    unit_decay = jnp.ones((head_count,), dtype=jnp.float32)
    zero_state = jnp.zeros((head_count, head_width, state_width), dtype=jnp.float32)
    fwd_decay, fwd_state = (unit_decay, zero_state)
    for entry in blocks:
        fwd_decay = fwd_decay * entry[6]
        fwd_state = entry[6][:, None, None] * fwd_state + entry[11]
    bwd_decay, bwd_state = (unit_decay, zero_state)
    for entry in reversed(blocks):
        bwd_decay = bwd_decay * entry[6]
        bwd_state = entry[12] + entry[6][:, None, None] * bwd_state
    state_in, grad_in = both_prefixes(fwd_decay, fwd_state, bwd_state, levels)
    entering = []
    current = state_in
    for entry in blocks:
        entering.append(current)
        current = entry[6][:, None, None] * current + entry[11]
    leaving = [None] * group_count
    current = grad_in
    for position in range(group_count - 1, -1, -1):
        leaving[position] = current
        current = blocks[position][12] + blocks[position][6][:, None, None] * current
    out_blocks, back_blocks, write_far, read_far = ([], [], [], [])
    for position in range(group_count):
        into_upstream, outof_scaled, write_part, read_part, into_factor, outof_factor = blocks[
            position
        ][:6]
        state_here = entering[position]
        state_after = leaving[position]
        out_blocks.append(
            blocks[position][7]
            + into_factor * jnp.einsum("tn,hpn->hpt", read_part, state_here, precision=highest)
        )
        back_blocks.append(
            blocks[position][8]
            + outof_factor * jnp.einsum("tn,hpn->hpt", write_part, state_after, precision=highest)
        )
        read_far.append(jnp.einsum("hpt,hpn->tn", into_upstream, state_here, precision=highest))
        write_far.append(jnp.einsum("hpt,hpn->tn", outof_scaled, state_after, precision=highest))
    result_rows = jnp.concatenate(out_blocks, axis=2)
    back_rows = jnp.concatenate(back_blocks, axis=2)
    write_carried = jnp.concatenate(write_far, axis=0)
    read_carried = jnp.concatenate(read_far, axis=0)
    write_total = jnp.concatenate([entry[9] for entry in blocks], axis=0) + write_carried
    read_total = jnp.concatenate([entry[10] for entry in blocks], axis=0) + read_carried
    both_grads = head_scatter(jnp.concatenate([write_total, read_total], axis=1), "head")
    write_grad, read_grad = (both_grads[:, :state_width], both_grads[:, state_width:])
    grad_input = (
        (step_size[:, None, :] * back_rows)
        .transpose(2, 0, 1)
        .reshape(row_count, head_count * head_width)
    )
    grad_step = jnp.sum(inputs * back_rows, axis=1)
    head_output = result_rows.transpose(2, 0, 1).reshape(row_count, head_count * head_width)
    return (head_output, grad_input, grad_step, write_grad, read_grad)


def solution(mesh):
    def run(*args):
        heads_here = args[1].shape[0] // mesh.shape["head"]
        ctx_count = mesh.shape["ctx"]
        inner = 1
        while inner < heads_here and inner < ctx_count and heads_here % (inner * 2) == 0:
            inner *= 2
        rest = ctx_count // inner
        factors = []
        while rest > 1:
            factor = 4 if rest % 4 == 0 else (2 if rest % 2 == 0 else rest)
            factors.append(factor)
            rest //= factor
        levels = tuple(f"level{k}" for k in range(len(factors)))
        fine = Mesh(
            mesh.devices.reshape(tuple(reversed(factors)) + (inner,) + mesh.devices.shape[1:]),
            tuple(reversed(levels)) + ("inner", "head"),
        )
        ctx = tuple(reversed(levels)) + ("inner",)
        placed = (
            P(ctx, "head"),
            P("head", ctx),
            P("head", ctx),
            P(ctx, None),
            P(ctx, None),
            P(ctx, "head"),
        )
        return jax.shard_map(
            functools.partial(shards, levels=levels),
            mesh=fine,
            in_specs=placed,
            out_specs=(
                P(ctx, "head"),
                P(ctx, "head"),
                P("head", ctx),
                P(ctx + ("head",), None),
                P(ctx + ("head",), None),
            ),
            check_vma=False,
        )(*args)

    return run
```

```python
import functools

import jax
import jax.numpy as jnp
from jax import lax
from jax.experimental import pallas as pl
from jax.experimental.pallas import tpu as pltpu
from jax.sharding import Mesh, PartitionSpec as P

GROUP = 128


def butterfly_rounds(shifts, size, here, span, before, after, final, axis):
    span_decay, span_fwd, span_bwd = span
    before_decay, before_state = before
    after_decay, after_state = after
    width = span_fwd.shape[1]
    extra = span_decay.shape[:1] + (1,) + span_fwd.shape[2:]
    for at, shift in enumerate(shifts):
        last = final and at == len(shifts) - 1
        upper = (here & shift) != 0
        pairs = [(j, j ^ shift) for j in range(size)]
        tail = jnp.broadcast_to(span_decay[:, None, None], extra)
        if last:
            packed = jnp.concatenate([jnp.where(upper, span_bwd, span_fwd), tail], axis=1)
        else:
            packed = jnp.concatenate([span_fwd, span_bwd, tail], axis=1)
        got = lax.ppermute(packed, axis, pairs)
        got_decay = got[:, -1, 0]
        if last:
            got_fwd = got_bwd = got[:, :width]
        else:
            got_fwd, got_bwd = (got[:, :width], got[:, width : 2 * width])
        scale = before_decay[:, None, None]
        before_state = jnp.where(upper, before_state + scale * got_fwd, before_state)
        before_decay = jnp.where(upper, before_decay * got_decay, before_decay)
        scale = after_decay[:, None, None]
        after_state = jnp.where(upper, after_state, after_state + scale * got_bwd)
        after_decay = jnp.where(upper, after_decay, after_decay * got_decay)
        if not last:
            mine = span_decay[:, None, None]
            theirs = got_decay[:, None, None]
            span_fwd = jnp.where(upper, span_fwd + mine * got_fwd, got_fwd + theirs * span_fwd)
            span_bwd = jnp.where(upper, got_bwd + theirs * span_bwd, span_bwd + mine * got_bwd)
            span_decay = span_decay * got_decay
    return ((span_decay, span_fwd, span_bwd), (before_decay, before_state), (after_decay, after_state))


INTERPRET = False


def level_kernel(count, width, last):
    rows = width + 1 if last else 2 * width + 1

    def kernel(here_ref, got_ref, *outs):
        here = here_ref[0]
        decays = [got_ref[s, rows - 1 : rows, :] for s in range(count)]
        fwds = [got_ref[s, 0:width, :] for s in range(count)]
        bwds = fwds if last else [got_ref[s, width : 2 * width, :] for s in range(count)]
        before_state = jnp.zeros((width, 128), jnp.float32)
        before_decay = jnp.ones((1, 128), jnp.float32)
        for s in range(count):
            take = s < here
            factor = jnp.where(take, decays[s], 1.0)
            before_state = factor * before_state + jnp.where(take, fwds[s], 0.0)
            before_decay = before_decay * factor
        after_state = jnp.zeros((width, 128), jnp.float32)
        after_decay = jnp.ones((1, 128), jnp.float32)
        for s in range(count - 1, -1, -1):
            take = s > here
            factor = jnp.where(take, decays[s], 1.0)
            after_state = jnp.where(take, bwds[s], 0.0) + factor * after_state
            after_decay = after_decay * factor
        outs[0][...] = before_state
        outs[1][...] = before_decay
        outs[2][...] = after_state
        outs[3][...] = after_decay
        if not last:
            span_fwd = jnp.zeros((width, 128), jnp.float32)
            span_decay = jnp.ones((1, 128), jnp.float32)
            for s in range(count):
                span_fwd = decays[s] * span_fwd + fwds[s]
                span_decay = span_decay * decays[s]
            span_bwd = jnp.zeros((width, 128), jnp.float32)
            for s in range(count - 1, -1, -1):
                span_bwd = bwds[s] + decays[s] * span_bwd
            outs[4][...] = span_fwd
            outs[5][...] = span_bwd
            outs[6][...] = span_decay

    state = jax.ShapeDtypeStruct((width, 128), jnp.float32)
    row = jax.ShapeDtypeStruct((1, 128), jnp.float32)
    shapes = (state, row, state, row) + (() if last else (state, state, row))
    vmem = pl.BlockSpec(memory_space=pltpu.VMEM)
    return pl.pallas_call(
        kernel,
        out_shape=shapes,
        in_specs=[pl.BlockSpec(memory_space=pltpu.SMEM), vmem],
        out_specs=tuple(vmem for _ in shapes),
        interpret=INTERPRET,
    )


def level_exchange(aggregate, axis, last):
    count, here = (lax.axis_size(axis), lax.axis_index(axis))
    tail, fwd, bwd = aggregate
    width = fwd.shape[1]
    if last:
        sent = jnp.stack(
            [jnp.concatenate([jnp.where(m < here, bwd, fwd), tail], axis=1) for m in range(count)]
        )
    else:
        packed = jnp.concatenate([fwd, bwd, tail], axis=1)
        sent = jnp.broadcast_to(packed[None], (count,) + packed.shape)
    got = lax.all_to_all(sent, axis, 0, 0)
    got = got.reshape((count,) + got.shape[2:])
    outs = level_kernel(count, width, last)(jnp.reshape(here, (1,)).astype(jnp.int32), got)
    if last:
        return (outs, None)
    return (outs[:4], (outs[6][None], outs[4][None], outs[5][None]))


def inner_kernel(members, width):
    def kernel(mine_ref, bs_ref, bd_ref, as_ref, ad_ref, sf_ref, sb_ref, sd_ref):
        rows = 2 * width + 1
        decays = [mine_ref[m, rows - 1 : rows, :] for m in range(members)]
        run_state = jnp.zeros((width, 128), jnp.float32)
        run_decay = jnp.ones((1, 128), jnp.float32)
        for m in range(members):
            bs_ref[m] = run_state
            bd_ref[m] = run_decay
            run_state = decays[m] * run_state + mine_ref[m, 0:width, :]
            run_decay = run_decay * decays[m]
        sf_ref[...] = run_state
        sd_ref[...] = run_decay
        run_state = jnp.zeros((width, 128), jnp.float32)
        run_decay = jnp.ones((1, 128), jnp.float32)
        for m in range(members - 1, -1, -1):
            as_ref[m] = run_state
            ad_ref[m] = run_decay
            run_state = mine_ref[m, width : 2 * width, :] + decays[m] * run_state
            run_decay = run_decay * decays[m]
        sb_ref[...] = run_state

    many = jax.ShapeDtypeStruct((members, width, 128), jnp.float32)
    many_rows = jax.ShapeDtypeStruct((members, 1, 128), jnp.float32)
    state = jax.ShapeDtypeStruct((width, 128), jnp.float32)
    row = jax.ShapeDtypeStruct((1, 128), jnp.float32)
    shapes = (many, many_rows, many, many_rows, state, state, row)
    vmem = pl.BlockSpec(memory_space=pltpu.VMEM)
    return pl.pallas_call(
        kernel, out_shape=shapes, in_specs=[vmem], out_specs=tuple(vmem for _ in shapes), interpret=INTERPRET
    )


def back_kernel(members, width, level_count):
    def kernel(*refs):
        bs_ref, bd_ref, as_ref, ad_ref = refs[:4]
        level_refs = refs[4 : 4 + 4 * level_count]
        out_ref = refs[-1]
        before_state = jnp.zeros((width, 128), jnp.float32)
        before_decay = jnp.ones((1, 128), jnp.float32)
        after_state = jnp.zeros((width, 128), jnp.float32)
        after_decay = jnp.ones((1, 128), jnp.float32)
        for k in range(level_count):
            lbs, lbd, las, lad = level_refs[4 * k : 4 * k + 4]
            before_state = before_state + before_decay * lbs[...]
            before_decay = before_decay * lbd[...]
            after_state = after_state + after_decay * las[...]
            after_decay = after_decay * lad[...]
        for m in range(members):
            out_ref[m, 0:width, :] = bs_ref[m] + bd_ref[m] * before_state
            out_ref[m, width : 2 * width, :] = as_ref[m] + ad_ref[m] * after_state

    vmem = pl.BlockSpec(memory_space=pltpu.VMEM)
    return pl.pallas_call(
        kernel,
        out_shape=jax.ShapeDtypeStruct((members, 2 * width, 128), jnp.float32),
        in_specs=[vmem] * (4 + 4 * level_count),
        out_specs=vmem,
        interpret=INTERPRET,
    )


def both_prefixes(decay, fwd_state, bwd_state, levels):
    members = lax.axis_size("inner")
    width = fwd_state.shape[1]
    packed = jnp.concatenate(
        [fwd_state, bwd_state, jnp.broadcast_to(decay[:, None, None], decay.shape[:1] + (1,) + fwd_state.shape[2:])],
        axis=1,
    )
    mine = lax.all_to_all(packed, "inner", 0, 0, tiled=True)
    prefixes = inner_kernel(members, width)(mine)
    aggregate = (prefixes[6][None], prefixes[4][None], prefixes[5][None])
    level_parts = []
    for at, axis in enumerate(levels):
        parts, aggregate = level_exchange(aggregate, axis, at == len(levels) - 1)
        level_parts += list(parts)
    back = back_kernel(members, width, len(levels))(*prefixes[:4], *level_parts)
    shared = lax.all_to_all(back, "inner", 0, 0, tiled=True)
    return (shared[:, :width], shared[:, width:])


def head_scatter(total, axis):
    size = lax.axis_size(axis)
    pieces = total.reshape((size, total.shape[0] // size) + total.shape[1:])
    return jnp.sum(lax.all_to_all(pieces, axis, 0, 0), axis=0)


def combine_forward(first_part, second_part):
    return (
        first_part[0] * second_part[0],
        second_part[1] + second_part[0][:, None, None] * first_part[1],
    )


def combine_backward(first_part, second_part):
    return (
        first_part[0] * second_part[0],
        second_part[1] + second_part[0][:, None, None] * first_part[1],
    )


def shards(head_input, step_size, log_decay, write_proj, read_proj, grad_out, levels):
    highest = lax.Precision.HIGHEST
    head_count = step_size.shape[0]
    row_count = head_input.shape[0]
    head_width = head_input.shape[1] // head_count
    state_width = write_proj.shape[1]
    group_count = row_count // GROUP
    inputs = head_input.reshape(row_count, head_count, head_width).transpose(1, 2, 0)
    scaled = inputs * step_size[:, None, :]
    upstream = grad_out.reshape(row_count, head_count, head_width).transpose(1, 2, 0)
    row_ids = lax.broadcasted_iota(jnp.int32, (GROUP, GROUP), 0)
    col_ids = lax.broadcasted_iota(jnp.int32, (GROUP, GROUP), 1)
    lower_mask = row_ids >= col_ids
    lower_ones = lower_mask.astype(jnp.float32)
    blocks = []
    for position in range(group_count):
        offset = position * GROUP
        group_rates = log_decay[:, offset : offset + GROUP]
        scaled_part = scaled[:, :, offset : offset + GROUP]
        upstream_part = upstream[:, :, offset : offset + GROUP]
        write_part = write_proj[offset : offset + GROUP]
        read_part = read_proj[offset : offset + GROUP]
        cumulated = jnp.dot(group_rates, lower_ones.T, precision=highest)
        final_cum = cumulated[:, -1:]
        gap_logs = cumulated[:, :, None] - cumulated[:, None, :]
        decay_mat = jnp.where(
            lower_mask[None], jnp.exp(jnp.where(lower_mask[None], gap_logs, 0.0)), 0.0
        )
        inner_prod = jnp.dot(read_part, write_part.T, precision=highest)
        mixed_mat = inner_prod[None] * decay_mat
        out_near = jnp.einsum("hts,hps->hpt", mixed_mat, scaled_part, precision=highest)
        back_near = jnp.einsum("hst,hps->hpt", mixed_mat, upstream_part, precision=highest)
        pair_prods = jnp.einsum("hpt,hps->hts", upstream_part, scaled_part, precision=highest)
        weight_sum = jnp.sum(decay_mat * pair_prods, axis=0)
        read_near = jnp.dot(weight_sum, write_part, precision=highest)
        write_near = jnp.dot(weight_sum.T, read_part, precision=highest)
        into_factor = jnp.exp(cumulated)[:, None, :]
        outof_factor = jnp.exp(final_cum - cumulated)[:, None, :]
        whole_decay = jnp.exp(final_cum[:, 0])
        into_upstream = into_factor * upstream_part
        outof_scaled = outof_factor * scaled_part
        fwd_part = jnp.einsum("hps,sn->hpn", outof_scaled, write_part, precision=highest)
        bwd_part = jnp.einsum("hps,sn->hpn", into_upstream, read_part, precision=highest)
        blocks.append(
            (
                into_upstream,
                outof_scaled,
                write_part,
                read_part,
                into_factor,
                outof_factor,
                whole_decay,
                out_near,
                back_near,
                write_near,
                read_near,
                fwd_part,
                bwd_part,
            )
        )
    unit_decay = jnp.ones((head_count,), dtype=jnp.float32)
    zero_state = jnp.zeros((head_count, head_width, state_width), dtype=jnp.float32)
    fwd_decay, fwd_state = (unit_decay, zero_state)
    for entry in blocks:
        fwd_decay = fwd_decay * entry[6]
        fwd_state = entry[6][:, None, None] * fwd_state + entry[11]
    bwd_decay, bwd_state = (unit_decay, zero_state)
    for entry in reversed(blocks):
        bwd_decay = bwd_decay * entry[6]
        bwd_state = entry[12] + entry[6][:, None, None] * bwd_state
    state_in, grad_in = both_prefixes(fwd_decay, fwd_state, bwd_state, levels)
    entering = []
    current = state_in
    for entry in blocks:
        entering.append(current)
        current = entry[6][:, None, None] * current + entry[11]
    leaving = [None] * group_count
    current = grad_in
    for position in range(group_count - 1, -1, -1):
        leaving[position] = current
        current = blocks[position][12] + blocks[position][6][:, None, None] * current
    out_blocks, back_blocks, write_far, read_far = ([], [], [], [])
    for position in range(group_count):
        into_upstream, outof_scaled, write_part, read_part, into_factor, outof_factor = blocks[
            position
        ][:6]
        state_here = entering[position]
        state_after = leaving[position]
        out_blocks.append(
            blocks[position][7]
            + into_factor * jnp.einsum("tn,hpn->hpt", read_part, state_here, precision=highest)
        )
        back_blocks.append(
            blocks[position][8]
            + outof_factor * jnp.einsum("tn,hpn->hpt", write_part, state_after, precision=highest)
        )
        read_far.append(jnp.einsum("hpt,hpn->tn", into_upstream, state_here, precision=highest))
        write_far.append(jnp.einsum("hpt,hpn->tn", outof_scaled, state_after, precision=highest))
    result_rows = jnp.concatenate(out_blocks, axis=2)
    back_rows = jnp.concatenate(back_blocks, axis=2)
    write_carried = jnp.concatenate(write_far, axis=0)
    read_carried = jnp.concatenate(read_far, axis=0)
    write_total = jnp.concatenate([entry[9] for entry in blocks], axis=0) + write_carried
    read_total = jnp.concatenate([entry[10] for entry in blocks], axis=0) + read_carried
    both_grads = head_scatter(jnp.concatenate([write_total, read_total], axis=1), "head")
    write_grad, read_grad = (both_grads[:, :state_width], both_grads[:, state_width:])
    grad_input = (
        (step_size[:, None, :] * back_rows)
        .transpose(2, 0, 1)
        .reshape(row_count, head_count * head_width)
    )
    grad_step = jnp.sum(inputs * back_rows, axis=1)
    head_output = result_rows.transpose(2, 0, 1).reshape(row_count, head_count * head_width)
    return (head_output, grad_input, grad_step, write_grad, read_grad)


def solution(mesh):
    def run(*args):
        heads_here = args[1].shape[0] // mesh.shape["head"]
        ctx_count = mesh.shape["ctx"]
        inner = 1
        while inner < heads_here and inner < ctx_count and heads_here % (inner * 2) == 0:
            inner *= 2
        rest = ctx_count // inner
        factors = []
        while rest > 1:
            factor = 4 if rest % 4 == 0 else (2 if rest % 2 == 0 else rest)
            factors.append(factor)
            rest //= factor
        levels = tuple(f"level{k}" for k in range(len(factors)))
        fine = Mesh(
            mesh.devices.reshape(tuple(reversed(factors)) + (inner,) + mesh.devices.shape[1:]),
            tuple(reversed(levels)) + ("inner", "head"),
        )
        ctx = tuple(reversed(levels)) + ("inner",)
        placed = (
            P(ctx, "head"),
            P("head", ctx),
            P("head", ctx),
            P(ctx, None),
            P(ctx, None),
            P(ctx, "head"),
        )
        return jax.shard_map(
            functools.partial(shards, levels=levels),
            mesh=fine,
            in_specs=placed,
            out_specs=(
                P(ctx, "head"),
                P(ctx, "head"),
                P("head", ctx),
                P(ctx + ("head",), None),
                P(ctx + ("head",), None),
            ),
            check_vma=False,
        )(*args)

    return run
```

```python
import functools
import math

import jax
import jax.numpy as jnp
from jax import lax
from jax.experimental import pallas as pl
from jax.experimental.pallas import tpu as pltpu
from jax.sharding import Mesh, PartitionSpec as P

GROUP = 128


def butterfly_rounds(shifts, size, here, span, before, after, final, axis):
    span_decay, span_fwd, span_bwd = span
    before_decay, before_state = before
    after_decay, after_state = after
    width = span_fwd.shape[1]
    extra = span_decay.shape[:1] + (1,) + span_fwd.shape[2:]
    for at, shift in enumerate(shifts):
        last = final and at == len(shifts) - 1
        upper = (here & shift) != 0
        pairs = [(j, j ^ shift) for j in range(size)]
        tail = jnp.broadcast_to(span_decay[:, None, None], extra)
        if last:
            packed = jnp.concatenate([jnp.where(upper, span_bwd, span_fwd), tail], axis=1)
        else:
            packed = jnp.concatenate([span_fwd, span_bwd, tail], axis=1)
        got = lax.ppermute(packed, axis, pairs)
        got_decay = got[:, -1, 0]
        if last:
            got_fwd = got_bwd = got[:, :width]
        else:
            got_fwd, got_bwd = (got[:, :width], got[:, width : 2 * width])
        scale = before_decay[:, None, None]
        before_state = jnp.where(upper, before_state + scale * got_fwd, before_state)
        before_decay = jnp.where(upper, before_decay * got_decay, before_decay)
        scale = after_decay[:, None, None]
        after_state = jnp.where(upper, after_state, after_state + scale * got_bwd)
        after_decay = jnp.where(upper, after_decay, after_decay * got_decay)
        if not last:
            mine = span_decay[:, None, None]
            theirs = got_decay[:, None, None]
            span_fwd = jnp.where(upper, span_fwd + mine * got_fwd, got_fwd + theirs * span_fwd)
            span_bwd = jnp.where(upper, got_bwd + theirs * span_bwd, span_bwd + mine * got_bwd)
            span_decay = span_decay * got_decay
    return ((span_decay, span_fwd, span_bwd), (before_decay, before_state), (after_decay, after_state))


INTERPRET = False


def level_kernel(count, width, last):
    rows = width + 1 if last else 2 * width + 1

    def kernel(here_ref, got_ref, *outs):
        here = here_ref[0]
        decays = [got_ref[s, rows - 1 : rows, :] for s in range(count)]
        fwds = [got_ref[s, 0:width, :] for s in range(count)]
        bwds = fwds if last else [got_ref[s, width : 2 * width, :] for s in range(count)]
        before_state = jnp.zeros((width, 128), jnp.float32)
        before_decay = jnp.ones((1, 128), jnp.float32)
        for s in range(count):
            take = s < here
            factor = jnp.where(take, decays[s], 1.0)
            before_state = factor * before_state + jnp.where(take, fwds[s], 0.0)
            before_decay = before_decay * factor
        after_state = jnp.zeros((width, 128), jnp.float32)
        after_decay = jnp.ones((1, 128), jnp.float32)
        for s in range(count - 1, -1, -1):
            take = s > here
            factor = jnp.where(take, decays[s], 1.0)
            after_state = jnp.where(take, bwds[s], 0.0) + factor * after_state
            after_decay = after_decay * factor
        outs[0][...] = before_state
        outs[1][...] = before_decay
        outs[2][...] = after_state
        outs[3][...] = after_decay
        if not last:
            span_fwd = jnp.zeros((width, 128), jnp.float32)
            span_decay = jnp.ones((1, 128), jnp.float32)
            for s in range(count):
                span_fwd = decays[s] * span_fwd + fwds[s]
                span_decay = span_decay * decays[s]
            span_bwd = jnp.zeros((width, 128), jnp.float32)
            for s in range(count - 1, -1, -1):
                span_bwd = bwds[s] + decays[s] * span_bwd
            outs[4][...] = span_fwd
            outs[5][...] = span_bwd
            outs[6][...] = span_decay

    state = jax.ShapeDtypeStruct((width, 128), jnp.float32)
    row = jax.ShapeDtypeStruct((1, 128), jnp.float32)
    shapes = (state, row, state, row) + (() if last else (state, state, row))
    vmem = pl.BlockSpec(memory_space=pltpu.VMEM)
    return pl.pallas_call(
        kernel,
        out_shape=shapes,
        in_specs=[pl.BlockSpec(memory_space=pltpu.SMEM), vmem],
        out_specs=tuple(vmem for _ in shapes),
        interpret=INTERPRET,
    )


def level_exchange(aggregate, axis, last):
    count, here = (lax.axis_size(axis), lax.axis_index(axis))
    tail, fwd, bwd = aggregate
    width = fwd.shape[1]
    if last:
        sent = jnp.stack(
            [jnp.concatenate([jnp.where(m < here, bwd, fwd), tail], axis=1) for m in range(count)]
        )
    else:
        packed = jnp.concatenate([fwd, bwd, tail], axis=1)
        sent = jnp.broadcast_to(packed[None], (count,) + packed.shape)
    got = lax.all_to_all(sent, axis, 0, 0)
    got = got.reshape((count,) + got.shape[2:])
    outs = level_kernel(count, width, last)(jnp.reshape(here, (1,)).astype(jnp.int32), got)
    if last:
        return (outs, None)
    return (outs[:4], (outs[6][None], outs[4][None], outs[5][None]))


def inner_kernel(members, width):
    def kernel(mine_ref, bs_ref, bd_ref, as_ref, ad_ref, sf_ref, sb_ref, sd_ref):
        rows = 2 * width + 1
        decays = [mine_ref[m, rows - 1 : rows, :] for m in range(members)]
        run_state = jnp.zeros((width, 128), jnp.float32)
        run_decay = jnp.ones((1, 128), jnp.float32)
        for m in range(members):
            bs_ref[m] = run_state
            bd_ref[m] = run_decay
            run_state = decays[m] * run_state + mine_ref[m, 0:width, :]
            run_decay = run_decay * decays[m]
        sf_ref[...] = run_state
        sd_ref[...] = run_decay
        run_state = jnp.zeros((width, 128), jnp.float32)
        run_decay = jnp.ones((1, 128), jnp.float32)
        for m in range(members - 1, -1, -1):
            as_ref[m] = run_state
            ad_ref[m] = run_decay
            run_state = mine_ref[m, width : 2 * width, :] + decays[m] * run_state
            run_decay = run_decay * decays[m]
        sb_ref[...] = run_state

    many = jax.ShapeDtypeStruct((members, width, 128), jnp.float32)
    many_rows = jax.ShapeDtypeStruct((members, 1, 128), jnp.float32)
    state = jax.ShapeDtypeStruct((width, 128), jnp.float32)
    row = jax.ShapeDtypeStruct((1, 128), jnp.float32)
    shapes = (many, many_rows, many, many_rows, state, state, row)
    vmem = pl.BlockSpec(memory_space=pltpu.VMEM)
    return pl.pallas_call(
        kernel, out_shape=shapes, in_specs=[vmem], out_specs=tuple(vmem for _ in shapes), interpret=INTERPRET
    )


def back_kernel(members, width, level_count):
    def kernel(*refs):
        bs_ref, bd_ref, as_ref, ad_ref = refs[:4]
        level_refs = refs[4 : 4 + 4 * level_count]
        out_ref = refs[-1]
        before_state = jnp.zeros((width, 128), jnp.float32)
        before_decay = jnp.ones((1, 128), jnp.float32)
        after_state = jnp.zeros((width, 128), jnp.float32)
        after_decay = jnp.ones((1, 128), jnp.float32)
        for k in range(level_count):
            lbs, lbd, las, lad = level_refs[4 * k : 4 * k + 4]
            before_state = before_state + before_decay * lbs[...]
            before_decay = before_decay * lbd[...]
            after_state = after_state + after_decay * las[...]
            after_decay = after_decay * lad[...]
        for m in range(members):
            out_ref[m, 0:width, :] = bs_ref[m] + bd_ref[m] * before_state
            out_ref[m, width : 2 * width, :] = as_ref[m] + ad_ref[m] * after_state

    vmem = pl.BlockSpec(memory_space=pltpu.VMEM)
    return pl.pallas_call(
        kernel,
        out_shape=jax.ShapeDtypeStruct((members, 2 * width, 128), jnp.float32),
        in_specs=[vmem] * (4 + 4 * level_count),
        out_specs=vmem,
        interpret=INTERPRET,
    )


def both_prefixes(decay, fwd_state, bwd_state, levels):
    members = lax.axis_size("inner")
    width = fwd_state.shape[1]
    packed = jnp.concatenate(
        [fwd_state, bwd_state, jnp.broadcast_to(decay[:, None, None], decay.shape[:1] + (1,) + fwd_state.shape[2:])],
        axis=1,
    )
    mine = lax.all_to_all(packed, "inner", 0, 0, tiled=True)
    prefixes = inner_kernel(members, width)(mine)
    aggregate = (prefixes[6][None], prefixes[4][None], prefixes[5][None])
    level_parts = []
    for at, axis in enumerate(levels):
        parts, aggregate = level_exchange(aggregate, axis, at == len(levels) - 1)
        level_parts += list(parts)
    back = back_kernel(members, width, len(levels))(*prefixes[:4], *level_parts)
    shared = lax.all_to_all(back, "inner", 0, 0, tiled=True)
    return (shared[:, :width], shared[:, width:])


def head_scatter(total, axes):
    sizes = [lax.axis_size(axis) for axis in axes]
    blocks = total.reshape(tuple(sizes) + (total.shape[0] // math.prod(sizes),) + total.shape[1:])
    for place in range(len(axes) - 1, -1, -1):
        blocks = jnp.sum(lax.all_to_all(blocks, axes[place], place, place, tiled=True), axis=place)
    return blocks


def combine_forward(first_part, second_part):
    return (
        first_part[0] * second_part[0],
        second_part[1] + second_part[0][:, None, None] * first_part[1],
    )


def combine_backward(first_part, second_part):
    return (
        first_part[0] * second_part[0],
        second_part[1] + second_part[0][:, None, None] * first_part[1],
    )


def shards(head_input, step_size, log_decay, write_proj, read_proj, grad_out, levels, head_axes):
    highest = lax.Precision.HIGHEST
    head_count = step_size.shape[0]
    row_count = head_input.shape[0]
    head_width = head_input.shape[1] // head_count
    state_width = write_proj.shape[1]
    group_count = row_count // GROUP
    inputs = head_input.reshape(row_count, head_count, head_width).transpose(1, 2, 0)
    scaled = inputs * step_size[:, None, :]
    upstream = grad_out.reshape(row_count, head_count, head_width).transpose(1, 2, 0)
    row_ids = lax.broadcasted_iota(jnp.int32, (GROUP, GROUP), 0)
    col_ids = lax.broadcasted_iota(jnp.int32, (GROUP, GROUP), 1)
    lower_mask = row_ids >= col_ids
    lower_ones = lower_mask.astype(jnp.float32)
    blocks = []
    for position in range(group_count):
        offset = position * GROUP
        group_rates = log_decay[:, offset : offset + GROUP]
        scaled_part = scaled[:, :, offset : offset + GROUP]
        upstream_part = upstream[:, :, offset : offset + GROUP]
        write_part = write_proj[offset : offset + GROUP]
        read_part = read_proj[offset : offset + GROUP]
        cumulated = jnp.dot(group_rates, lower_ones.T, precision=highest)
        final_cum = cumulated[:, -1:]
        gap_logs = cumulated[:, :, None] - cumulated[:, None, :]
        decay_mat = jnp.where(
            lower_mask[None], jnp.exp(jnp.where(lower_mask[None], gap_logs, 0.0)), 0.0
        )
        inner_prod = jnp.dot(read_part, write_part.T, precision=highest)
        mixed_mat = inner_prod[None] * decay_mat
        out_near = jnp.einsum("hts,hps->hpt", mixed_mat, scaled_part, precision=highest)
        back_near = jnp.einsum("hst,hps->hpt", mixed_mat, upstream_part, precision=highest)
        pair_prods = jnp.einsum("hpt,hps->hts", upstream_part, scaled_part, precision=highest)
        weight_sum = jnp.sum(decay_mat * pair_prods, axis=0)
        read_near = jnp.dot(weight_sum, write_part, precision=highest)
        write_near = jnp.dot(weight_sum.T, read_part, precision=highest)
        into_factor = jnp.exp(cumulated)[:, None, :]
        outof_factor = jnp.exp(final_cum - cumulated)[:, None, :]
        whole_decay = jnp.exp(final_cum[:, 0])
        into_upstream = into_factor * upstream_part
        outof_scaled = outof_factor * scaled_part
        fwd_part = jnp.einsum("hps,sn->hpn", outof_scaled, write_part, precision=highest)
        bwd_part = jnp.einsum("hps,sn->hpn", into_upstream, read_part, precision=highest)
        blocks.append(
            (
                into_upstream,
                outof_scaled,
                write_part,
                read_part,
                into_factor,
                outof_factor,
                whole_decay,
                out_near,
                back_near,
                write_near,
                read_near,
                fwd_part,
                bwd_part,
            )
        )
    unit_decay = jnp.ones((head_count,), dtype=jnp.float32)
    zero_state = jnp.zeros((head_count, head_width, state_width), dtype=jnp.float32)
    fwd_decay, fwd_state = (unit_decay, zero_state)
    for entry in blocks:
        fwd_decay = fwd_decay * entry[6]
        fwd_state = entry[6][:, None, None] * fwd_state + entry[11]
    bwd_decay, bwd_state = (unit_decay, zero_state)
    for entry in reversed(blocks):
        bwd_decay = bwd_decay * entry[6]
        bwd_state = entry[12] + entry[6][:, None, None] * bwd_state
    state_in, grad_in = both_prefixes(fwd_decay, fwd_state, bwd_state, levels)
    entering = []
    current = state_in
    for entry in blocks:
        entering.append(current)
        current = entry[6][:, None, None] * current + entry[11]
    leaving = [None] * group_count
    current = grad_in
    for position in range(group_count - 1, -1, -1):
        leaving[position] = current
        current = blocks[position][12] + blocks[position][6][:, None, None] * current
    out_blocks, back_blocks, write_far, read_far = ([], [], [], [])
    for position in range(group_count):
        into_upstream, outof_scaled, write_part, read_part, into_factor, outof_factor = blocks[
            position
        ][:6]
        state_here = entering[position]
        state_after = leaving[position]
        out_blocks.append(
            blocks[position][7]
            + into_factor * jnp.einsum("tn,hpn->hpt", read_part, state_here, precision=highest)
        )
        back_blocks.append(
            blocks[position][8]
            + outof_factor * jnp.einsum("tn,hpn->hpt", write_part, state_after, precision=highest)
        )
        read_far.append(jnp.einsum("hpt,hpn->tn", into_upstream, state_here, precision=highest))
        write_far.append(jnp.einsum("hpt,hpn->tn", outof_scaled, state_after, precision=highest))
    result_rows = jnp.concatenate(out_blocks, axis=2)
    back_rows = jnp.concatenate(back_blocks, axis=2)
    write_carried = jnp.concatenate(write_far, axis=0)
    read_carried = jnp.concatenate(read_far, axis=0)
    write_total = jnp.concatenate([entry[9] for entry in blocks], axis=0) + write_carried
    read_total = jnp.concatenate([entry[10] for entry in blocks], axis=0) + read_carried
    both_grads = head_scatter(jnp.concatenate([write_total, read_total], axis=1), head_axes)
    write_grad, read_grad = (both_grads[:, :state_width], both_grads[:, state_width:])
    grad_input = (
        (step_size[:, None, :] * back_rows)
        .transpose(2, 0, 1)
        .reshape(row_count, head_count * head_width)
    )
    grad_step = jnp.sum(inputs * back_rows, axis=1)
    head_output = result_rows.transpose(2, 0, 1).reshape(row_count, head_count * head_width)
    return (head_output, grad_input, grad_step, write_grad, read_grad)


def solution(mesh):
    def run(*args):
        heads_here = args[1].shape[0] // mesh.shape["head"]
        ctx_count = mesh.shape["ctx"]
        inner = 1
        while inner < heads_here and inner < ctx_count and heads_here % (inner * 2) == 0:
            inner *= 2
        rest = ctx_count // inner
        factors = []
        while rest > 1:
            factor = 4 if rest % 4 == 0 else (2 if rest % 2 == 0 else rest)
            factors.append(factor)
            rest //= factor
        levels = tuple(f"level{k}" for k in range(len(factors)))
        head_count = mesh.shape["head"]
        pair = 2 if head_count % 2 == 0 else 1
        head_axes = ("head_outer", "head_inner")
        fine = Mesh(
            mesh.devices.reshape(tuple(reversed(factors)) + (inner, head_count // pair, pair)),
            tuple(reversed(levels)) + ("inner",) + head_axes,
        )
        head = head_axes
        ctx = tuple(reversed(levels)) + ("inner",)
        placed = (
            P(ctx, head),
            P(head, ctx),
            P(head, ctx),
            P(ctx, None),
            P(ctx, None),
            P(ctx, head),
        )
        return jax.shard_map(
            functools.partial(shards, levels=levels, head_axes=head_axes),
            mesh=fine,
            in_specs=placed,
            out_specs=(
                P(ctx, head),
                P(ctx, head),
                P(head, ctx),
                P(ctx + head, None),
                P(ctx + head, None),
            ),
            check_vma=False,
        )(*args)

    return run
```

```python
import functools
import math

import jax
import jax.numpy as jnp
from jax import lax
from jax.experimental import pallas as pl
from jax.experimental.pallas import tpu as pltpu
from jax.sharding import Mesh, PartitionSpec as P

GROUP = 128


def butterfly_rounds(shifts, size, here, span, before, after, final, axis):
    span_decay, span_fwd, span_bwd = span
    before_decay, before_state = before
    after_decay, after_state = after
    width = span_fwd.shape[1]
    extra = span_decay.shape[:1] + (1,) + span_fwd.shape[2:]
    for at, shift in enumerate(shifts):
        last = final and at == len(shifts) - 1
        upper = (here & shift) != 0
        pairs = [(j, j ^ shift) for j in range(size)]
        tail = jnp.broadcast_to(span_decay[:, None, None], extra)
        if last:
            packed = jnp.concatenate([jnp.where(upper, span_bwd, span_fwd), tail], axis=1)
        else:
            packed = jnp.concatenate([span_fwd, span_bwd, tail], axis=1)
        got = lax.ppermute(packed, axis, pairs)
        got_decay = got[:, -1, 0]
        if last:
            got_fwd = got_bwd = got[:, :width]
        else:
            got_fwd, got_bwd = (got[:, :width], got[:, width : 2 * width])
        scale = before_decay[:, None, None]
        before_state = jnp.where(upper, before_state + scale * got_fwd, before_state)
        before_decay = jnp.where(upper, before_decay * got_decay, before_decay)
        scale = after_decay[:, None, None]
        after_state = jnp.where(upper, after_state, after_state + scale * got_bwd)
        after_decay = jnp.where(upper, after_decay, after_decay * got_decay)
        if not last:
            mine = span_decay[:, None, None]
            theirs = got_decay[:, None, None]
            span_fwd = jnp.where(upper, span_fwd + mine * got_fwd, got_fwd + theirs * span_fwd)
            span_bwd = jnp.where(upper, got_bwd + theirs * span_bwd, span_bwd + mine * got_bwd)
            span_decay = span_decay * got_decay
    return ((span_decay, span_fwd, span_bwd), (before_decay, before_state), (after_decay, after_state))


INTERPRET = False


def level_kernel(count, width, last):
    rows = width + 1 if last else 2 * width + 1

    def kernel(here_ref, got_ref, *outs):
        here = here_ref[0]
        decays = [got_ref[s, rows - 1 : rows, :] for s in range(count)]
        fwds = [got_ref[s, 0:width, :] for s in range(count)]
        bwds = fwds if last else [got_ref[s, width : 2 * width, :] for s in range(count)]
        before_state = jnp.zeros((width, 128), jnp.float32)
        before_decay = jnp.ones((1, 128), jnp.float32)
        for s in range(count):
            take = s < here
            factor = jnp.where(take, decays[s], 1.0)
            before_state = factor * before_state + jnp.where(take, fwds[s], 0.0)
            before_decay = before_decay * factor
        after_state = jnp.zeros((width, 128), jnp.float32)
        after_decay = jnp.ones((1, 128), jnp.float32)
        for s in range(count - 1, -1, -1):
            take = s > here
            factor = jnp.where(take, decays[s], 1.0)
            after_state = jnp.where(take, bwds[s], 0.0) + factor * after_state
            after_decay = after_decay * factor
        outs[0][...] = before_state
        outs[1][...] = before_decay
        outs[2][...] = after_state
        outs[3][...] = after_decay
        if not last:
            span_fwd = jnp.zeros((width, 128), jnp.float32)
            span_decay = jnp.ones((1, 128), jnp.float32)
            for s in range(count):
                span_fwd = decays[s] * span_fwd + fwds[s]
                span_decay = span_decay * decays[s]
            span_bwd = jnp.zeros((width, 128), jnp.float32)
            for s in range(count - 1, -1, -1):
                span_bwd = bwds[s] + decays[s] * span_bwd
            outs[4][...] = span_fwd
            outs[5][...] = span_bwd
            outs[6][...] = span_decay

    state = jax.ShapeDtypeStruct((width, 128), jnp.float32)
    row = jax.ShapeDtypeStruct((1, 128), jnp.float32)
    shapes = (state, row, state, row) + (() if last else (state, state, row))
    vmem = pl.BlockSpec(memory_space=pltpu.VMEM)
    return pl.pallas_call(
        kernel,
        out_shape=shapes,
        in_specs=[pl.BlockSpec(memory_space=pltpu.SMEM), vmem],
        out_specs=tuple(vmem for _ in shapes),
        interpret=INTERPRET,
    )


def level_exchange(aggregate, axis, last):
    count, here = (lax.axis_size(axis), lax.axis_index(axis))
    tail, fwd, bwd = aggregate
    width = fwd.shape[1]
    if last:
        sent = jnp.stack(
            [jnp.concatenate([jnp.where(m < here, bwd, fwd), tail], axis=1) for m in range(count)]
        )
    else:
        packed = jnp.concatenate([fwd, bwd, tail], axis=1)
        sent = jnp.broadcast_to(packed[None], (count,) + packed.shape)
    got = lax.all_to_all(sent, axis, 0, 0)
    got = got.reshape((count,) + got.shape[2:])
    outs = level_kernel(count, width, last)(jnp.reshape(here, (1,)).astype(jnp.int32), got)
    if last:
        return (outs, None)
    return (outs[:4], (outs[6][None], outs[4][None], outs[5][None]))


def inner_kernel(members, width):
    def kernel(mine_ref, bs_ref, bd_ref, as_ref, ad_ref, sf_ref, sb_ref, sd_ref):
        rows = 2 * width + 1
        decays = [mine_ref[m, rows - 1 : rows, :] for m in range(members)]
        run_state = jnp.zeros((width, 128), jnp.float32)
        run_decay = jnp.ones((1, 128), jnp.float32)
        for m in range(members):
            bs_ref[m] = run_state
            bd_ref[m] = run_decay
            run_state = decays[m] * run_state + mine_ref[m, 0:width, :]
            run_decay = run_decay * decays[m]
        sf_ref[...] = run_state
        sd_ref[...] = run_decay
        run_state = jnp.zeros((width, 128), jnp.float32)
        run_decay = jnp.ones((1, 128), jnp.float32)
        for m in range(members - 1, -1, -1):
            as_ref[m] = run_state
            ad_ref[m] = run_decay
            run_state = mine_ref[m, width : 2 * width, :] + decays[m] * run_state
            run_decay = run_decay * decays[m]
        sb_ref[...] = run_state

    many = jax.ShapeDtypeStruct((members, width, 128), jnp.float32)
    many_rows = jax.ShapeDtypeStruct((members, 1, 128), jnp.float32)
    state = jax.ShapeDtypeStruct((width, 128), jnp.float32)
    row = jax.ShapeDtypeStruct((1, 128), jnp.float32)
    shapes = (many, many_rows, many, many_rows, state, state, row)
    vmem = pl.BlockSpec(memory_space=pltpu.VMEM)
    return pl.pallas_call(
        kernel, out_shape=shapes, in_specs=[vmem], out_specs=tuple(vmem for _ in shapes), interpret=INTERPRET
    )


def back_kernel(members, width, level_count):
    def kernel(*refs):
        bs_ref, bd_ref, as_ref, ad_ref = refs[:4]
        level_refs = refs[4 : 4 + 4 * level_count]
        out_ref = refs[-1]
        before_state = jnp.zeros((width, 128), jnp.float32)
        before_decay = jnp.ones((1, 128), jnp.float32)
        after_state = jnp.zeros((width, 128), jnp.float32)
        after_decay = jnp.ones((1, 128), jnp.float32)
        for k in range(level_count):
            lbs, lbd, las, lad = level_refs[4 * k : 4 * k + 4]
            before_state = before_state + before_decay * lbs[...]
            before_decay = before_decay * lbd[...]
            after_state = after_state + after_decay * las[...]
            after_decay = after_decay * lad[...]
        for m in range(members):
            out_ref[m, 0:width, :] = bs_ref[m] + bd_ref[m] * before_state
            out_ref[m, width : 2 * width, :] = as_ref[m] + ad_ref[m] * after_state

    vmem = pl.BlockSpec(memory_space=pltpu.VMEM)
    return pl.pallas_call(
        kernel,
        out_shape=jax.ShapeDtypeStruct((members, 2 * width, 128), jnp.float32),
        in_specs=[vmem] * (4 + 4 * level_count),
        out_specs=vmem,
        interpret=INTERPRET,
    )


def both_prefixes(decay, fwd_state, bwd_state, levels):
    members = lax.axis_size("inner")
    width = fwd_state.shape[1]
    packed = jnp.concatenate(
        [fwd_state, bwd_state, jnp.broadcast_to(decay[:, None, None], decay.shape[:1] + (1,) + fwd_state.shape[2:])],
        axis=1,
    )
    mine = lax.all_to_all(packed, "inner", 0, 0, tiled=True)
    prefixes = inner_kernel(members, width)(mine)
    aggregate = (prefixes[6][None], prefixes[4][None], prefixes[5][None])
    level_parts = []
    for at, axis in enumerate(levels):
        parts, aggregate = level_exchange(aggregate, axis, at == len(levels) - 1)
        level_parts += list(parts)
    back = back_kernel(members, width, len(levels))(*prefixes[:4], *level_parts)
    shared = lax.all_to_all(back, "inner", 0, 0, tiled=True)
    return (shared[:, :width], shared[:, width:])


def head_scatter(total, axes):
    sizes = [lax.axis_size(axis) for axis in axes]
    blocks = total.reshape(tuple(sizes) + (total.shape[0] // math.prod(sizes),) + total.shape[1:])
    for place in range(len(axes) - 1, -1, -1):
        blocks = jnp.sum(lax.all_to_all(blocks, axes[place], place, place, tiled=True), axis=place)
    return blocks


def combine_forward(first_part, second_part):
    return (
        first_part[0] * second_part[0],
        second_part[1] + second_part[0][:, None, None] * first_part[1],
    )


def combine_backward(first_part, second_part):
    return (
        first_part[0] * second_part[0],
        second_part[1] + second_part[0][:, None, None] * first_part[1],
    )


def shards(head_input, step_size, log_decay, write_proj, read_proj, grad_out, levels, head_axes):
    highest = lax.Precision.HIGHEST
    head_count = step_size.shape[0]
    row_count = head_input.shape[0]
    head_width = head_input.shape[1] // head_count
    state_width = write_proj.shape[1]
    group_count = row_count // GROUP
    inputs = head_input.reshape(row_count, head_count, head_width).transpose(1, 2, 0)
    scaled = inputs * step_size[:, None, :]
    upstream = grad_out.reshape(row_count, head_count, head_width).transpose(1, 2, 0)
    row_ids = lax.broadcasted_iota(jnp.int32, (GROUP, GROUP), 0)
    col_ids = lax.broadcasted_iota(jnp.int32, (GROUP, GROUP), 1)
    lower_mask = row_ids >= col_ids
    lower_ones = lower_mask.astype(jnp.float32)
    blocks = []
    for position in range(group_count):
        offset = position * GROUP
        group_rates = log_decay[:, offset : offset + GROUP]
        scaled_part = scaled[:, :, offset : offset + GROUP]
        upstream_part = upstream[:, :, offset : offset + GROUP]
        write_part = write_proj[offset : offset + GROUP]
        read_part = read_proj[offset : offset + GROUP]
        cumulated = jnp.dot(group_rates, lower_ones.T, precision=highest)
        final_cum = cumulated[:, -1:]
        gap_logs = cumulated[:, :, None] - cumulated[:, None, :]
        decay_mat = jnp.where(
            lower_mask[None], jnp.exp(jnp.where(lower_mask[None], gap_logs, 0.0)), 0.0
        )
        inner_prod = jnp.dot(read_part, write_part.T, precision=highest)
        mixed_mat = inner_prod[None] * decay_mat
        out_near = jnp.einsum("hts,hps->hpt", mixed_mat, scaled_part, precision=highest)
        back_near = jnp.einsum("hst,hps->hpt", mixed_mat, upstream_part, precision=highest)
        pair_prods = jnp.einsum("hpt,hps->hts", upstream_part, scaled_part, precision=highest)
        weight_sum = jnp.sum(decay_mat * pair_prods, axis=0)
        read_near = jnp.dot(weight_sum, write_part, precision=highest)
        write_near = jnp.dot(weight_sum.T, read_part, precision=highest)
        into_factor = jnp.exp(cumulated)[:, None, :]
        outof_factor = jnp.exp(final_cum - cumulated)[:, None, :]
        whole_decay = jnp.exp(final_cum[:, 0])
        into_upstream = into_factor * upstream_part
        outof_scaled = outof_factor * scaled_part
        fwd_part = jnp.einsum("hps,sn->hpn", outof_scaled, write_part, precision=highest)
        bwd_part = jnp.einsum("hps,sn->hpn", into_upstream, read_part, precision=highest)
        blocks.append(
            (
                into_upstream,
                outof_scaled,
                write_part,
                read_part,
                into_factor,
                outof_factor,
                whole_decay,
                out_near,
                back_near,
                write_near,
                read_near,
                fwd_part,
                bwd_part,
            )
        )
    block_cum = jnp.dot(
        log_decay.reshape(head_count * group_count, GROUP), lower_ones.T, precision=highest
    ).reshape(head_count, group_count, GROUP)
    block_final = block_cum[:, :, -1:]
    block_decay = jnp.exp(block_final)
    later = [None] * group_count
    earlier = [None] * group_count
    running = jnp.ones((head_count, 1), jnp.float32)
    for position in range(group_count - 1, -1, -1):
        later[position] = running
        running = running * block_decay[:, position]
    fwd_decay = running[:, 0]
    running = jnp.ones((head_count, 1), jnp.float32)
    for position in range(group_count):
        earlier[position] = running
        running = running * block_decay[:, position]
    fwd_weight = jnp.concatenate(
        [later[b] * jnp.exp(block_final[:, b] - block_cum[:, b]) for b in range(group_count)], axis=1
    )
    bwd_weight = jnp.concatenate(
        [earlier[b] * jnp.exp(block_cum[:, b]) for b in range(group_count)], axis=1
    )
    fwd_rows = head_input.reshape(row_count, head_count, head_width) * (step_size * fwd_weight).T[:, :, None]
    fwd_state = jnp.einsum("thp,tn->hpn", fwd_rows, write_proj, precision=highest)
    bwd_rows = grad_out.reshape(row_count, head_count, head_width) * bwd_weight.T[:, :, None]
    bwd_state = jnp.einsum("thp,tn->hpn", bwd_rows, read_proj, precision=highest)
    state_in, grad_in = both_prefixes(fwd_decay, fwd_state, bwd_state, levels)
    entering = []
    current = state_in
    for entry in blocks:
        entering.append(current)
        current = entry[6][:, None, None] * current + entry[11]
    leaving = [None] * group_count
    current = grad_in
    for position in range(group_count - 1, -1, -1):
        leaving[position] = current
        current = blocks[position][12] + blocks[position][6][:, None, None] * current
    out_blocks, back_blocks, write_far, read_far = ([], [], [], [])
    for position in range(group_count):
        into_upstream, outof_scaled, write_part, read_part, into_factor, outof_factor = blocks[
            position
        ][:6]
        state_here = entering[position]
        state_after = leaving[position]
        out_blocks.append(
            blocks[position][7]
            + into_factor * jnp.einsum("tn,hpn->hpt", read_part, state_here, precision=highest)
        )
        back_blocks.append(
            blocks[position][8]
            + outof_factor * jnp.einsum("tn,hpn->hpt", write_part, state_after, precision=highest)
        )
        read_far.append(jnp.einsum("hpt,hpn->tn", into_upstream, state_here, precision=highest))
        write_far.append(jnp.einsum("hpt,hpn->tn", outof_scaled, state_after, precision=highest))
    result_rows = jnp.concatenate(out_blocks, axis=2)
    back_rows = jnp.concatenate(back_blocks, axis=2)
    write_carried = jnp.concatenate(write_far, axis=0)
    read_carried = jnp.concatenate(read_far, axis=0)
    write_total = jnp.concatenate([entry[9] for entry in blocks], axis=0) + write_carried
    read_total = jnp.concatenate([entry[10] for entry in blocks], axis=0) + read_carried
    both_grads = head_scatter(jnp.concatenate([write_total, read_total], axis=1), head_axes)
    write_grad, read_grad = (both_grads[:, :state_width], both_grads[:, state_width:])
    grad_input = (
        (step_size[:, None, :] * back_rows)
        .transpose(2, 0, 1)
        .reshape(row_count, head_count * head_width)
    )
    grad_step = jnp.sum(inputs * back_rows, axis=1)
    head_output = result_rows.transpose(2, 0, 1).reshape(row_count, head_count * head_width)
    return (head_output, grad_input, grad_step, write_grad, read_grad)


def solution(mesh):
    def run(*args):
        heads_here = args[1].shape[0] // mesh.shape["head"]
        ctx_count = mesh.shape["ctx"]
        inner = 1
        while inner < heads_here and inner < ctx_count and heads_here % (inner * 2) == 0:
            inner *= 2
        rest = ctx_count // inner
        factors = []
        while rest > 1:
            factor = 4 if rest % 4 == 0 else (2 if rest % 2 == 0 else rest)
            factors.append(factor)
            rest //= factor
        levels = tuple(f"level{k}" for k in range(len(factors)))
        head_count = mesh.shape["head"]
        pair = 2 if head_count % 2 == 0 else 1
        head_axes = ("head_outer", "head_inner")
        fine = Mesh(
            mesh.devices.reshape(tuple(reversed(factors)) + (inner, head_count // pair, pair)),
            tuple(reversed(levels)) + ("inner",) + head_axes,
        )
        head = head_axes
        ctx = tuple(reversed(levels)) + ("inner",)
        placed = (
            P(ctx, head),
            P(head, ctx),
            P(head, ctx),
            P(ctx, None),
            P(ctx, None),
            P(ctx, head),
        )
        return jax.shard_map(
            functools.partial(shards, levels=levels, head_axes=head_axes),
            mesh=fine,
            in_specs=placed,
            out_specs=(
                P(ctx, head),
                P(ctx, head),
                P(head, ctx),
                P(ctx + head, None),
                P(ctx + head, None),
            ),
            check_vma=False,
        )(*args)

    return run
```

```python
import functools
import math

import jax
import jax.numpy as jnp
from jax import lax
from jax.experimental import pallas as pl
from jax.experimental.pallas import tpu as pltpu
from jax.sharding import Mesh, PartitionSpec as P

GROUP = 128


def butterfly_rounds(shifts, size, here, span, before, after, final, axis):
    span_decay, span_fwd, span_bwd = span
    before_decay, before_state = before
    after_decay, after_state = after
    width = span_fwd.shape[1]
    extra = span_decay.shape[:1] + (1,) + span_fwd.shape[2:]
    for at, shift in enumerate(shifts):
        last = final and at == len(shifts) - 1
        upper = (here & shift) != 0
        pairs = [(j, j ^ shift) for j in range(size)]
        tail = jnp.broadcast_to(span_decay[:, None, None], extra)
        if last:
            packed = jnp.concatenate([jnp.where(upper, span_bwd, span_fwd), tail], axis=1)
        else:
            packed = jnp.concatenate([span_fwd, span_bwd, tail], axis=1)
        got = lax.ppermute(packed, axis, pairs)
        got_decay = got[:, -1, 0]
        if last:
            got_fwd = got_bwd = got[:, :width]
        else:
            got_fwd, got_bwd = (got[:, :width], got[:, width : 2 * width])
        scale = before_decay[:, None, None]
        before_state = jnp.where(upper, before_state + scale * got_fwd, before_state)
        before_decay = jnp.where(upper, before_decay * got_decay, before_decay)
        scale = after_decay[:, None, None]
        after_state = jnp.where(upper, after_state, after_state + scale * got_bwd)
        after_decay = jnp.where(upper, after_decay, after_decay * got_decay)
        if not last:
            mine = span_decay[:, None, None]
            theirs = got_decay[:, None, None]
            span_fwd = jnp.where(upper, span_fwd + mine * got_fwd, got_fwd + theirs * span_fwd)
            span_bwd = jnp.where(upper, got_bwd + theirs * span_bwd, span_bwd + mine * got_bwd)
            span_decay = span_decay * got_decay
    return ((span_decay, span_fwd, span_bwd), (before_decay, before_state), (after_decay, after_state))


INTERPRET = False


def level_kernel(count, width, last):
    rows = width + 1 if last else 2 * width + 1

    def kernel(here_ref, got_ref, *outs):
        here = here_ref[0]
        decays = [got_ref[s, rows - 1 : rows, :] for s in range(count)]
        fwds = [got_ref[s, 0:width, :] for s in range(count)]
        bwds = fwds if last else [got_ref[s, width : 2 * width, :] for s in range(count)]
        before_state = jnp.zeros((width, 128), jnp.float32)
        before_decay = jnp.ones((1, 128), jnp.float32)
        for s in range(count):
            take = s < here
            factor = jnp.where(take, decays[s], 1.0)
            before_state = factor * before_state + jnp.where(take, fwds[s], 0.0)
            before_decay = before_decay * factor
        after_state = jnp.zeros((width, 128), jnp.float32)
        after_decay = jnp.ones((1, 128), jnp.float32)
        for s in range(count - 1, -1, -1):
            take = s > here
            factor = jnp.where(take, decays[s], 1.0)
            after_state = jnp.where(take, bwds[s], 0.0) + factor * after_state
            after_decay = after_decay * factor
        outs[0][...] = before_state
        outs[1][...] = before_decay
        outs[2][...] = after_state
        outs[3][...] = after_decay
        if not last:
            span_fwd = jnp.zeros((width, 128), jnp.float32)
            span_decay = jnp.ones((1, 128), jnp.float32)
            for s in range(count):
                span_fwd = decays[s] * span_fwd + fwds[s]
                span_decay = span_decay * decays[s]
            span_bwd = jnp.zeros((width, 128), jnp.float32)
            for s in range(count - 1, -1, -1):
                span_bwd = bwds[s] + decays[s] * span_bwd
            outs[4][...] = span_fwd
            outs[5][...] = span_bwd
            outs[6][...] = span_decay

    state = jax.ShapeDtypeStruct((width, 128), jnp.float32)
    row = jax.ShapeDtypeStruct((1, 128), jnp.float32)
    shapes = (state, row, state, row) + (() if last else (state, state, row))
    vmem = pl.BlockSpec(memory_space=pltpu.VMEM)
    return pl.pallas_call(
        kernel,
        out_shape=shapes,
        in_specs=[pl.BlockSpec(memory_space=pltpu.SMEM), vmem],
        out_specs=tuple(vmem for _ in shapes),
        interpret=INTERPRET,
    )


def level_exchange(aggregate, axis, last):
    count, here = (lax.axis_size(axis), lax.axis_index(axis))
    tail, fwd, bwd = aggregate
    width = fwd.shape[1]
    if last:
        sent = jnp.stack(
            [jnp.concatenate([jnp.where(m < here, bwd, fwd), tail], axis=1) for m in range(count)]
        )
    else:
        packed = jnp.concatenate([fwd, bwd, tail], axis=1)
        sent = jnp.broadcast_to(packed[None], (count,) + packed.shape)
    got = lax.all_to_all(sent, axis, 0, 0)
    got = got.reshape((count,) + got.shape[2:])
    outs = level_kernel(count, width, last)(jnp.reshape(here, (1,)).astype(jnp.int32), got)
    if last:
        return (outs, None)
    return (outs[:4], (outs[6][None], outs[4][None], outs[5][None]))


def inner_kernel(members, width):
    def kernel(mine_ref, bs_ref, bd_ref, as_ref, ad_ref, sf_ref, sb_ref, sd_ref):
        rows = 2 * width + 1
        decays = [mine_ref[m, rows - 1 : rows, :] for m in range(members)]
        run_state = jnp.zeros((width, 128), jnp.float32)
        run_decay = jnp.ones((1, 128), jnp.float32)
        for m in range(members):
            bs_ref[m] = run_state
            bd_ref[m] = run_decay
            run_state = decays[m] * run_state + mine_ref[m, 0:width, :]
            run_decay = run_decay * decays[m]
        sf_ref[...] = run_state
        sd_ref[...] = run_decay
        run_state = jnp.zeros((width, 128), jnp.float32)
        run_decay = jnp.ones((1, 128), jnp.float32)
        for m in range(members - 1, -1, -1):
            as_ref[m] = run_state
            ad_ref[m] = run_decay
            run_state = mine_ref[m, width : 2 * width, :] + decays[m] * run_state
            run_decay = run_decay * decays[m]
        sb_ref[...] = run_state

    many = jax.ShapeDtypeStruct((members, width, 128), jnp.float32)
    many_rows = jax.ShapeDtypeStruct((members, 1, 128), jnp.float32)
    state = jax.ShapeDtypeStruct((width, 128), jnp.float32)
    row = jax.ShapeDtypeStruct((1, 128), jnp.float32)
    shapes = (many, many_rows, many, many_rows, state, state, row)
    vmem = pl.BlockSpec(memory_space=pltpu.VMEM)
    return pl.pallas_call(
        kernel, out_shape=shapes, in_specs=[vmem], out_specs=tuple(vmem for _ in shapes), interpret=INTERPRET
    )


def back_kernel(members, width, level_count):
    def kernel(*refs):
        bs_ref, bd_ref, as_ref, ad_ref = refs[:4]
        level_refs = refs[4 : 4 + 4 * level_count]
        out_ref = refs[-1]
        before_state = jnp.zeros((width, 128), jnp.float32)
        before_decay = jnp.ones((1, 128), jnp.float32)
        after_state = jnp.zeros((width, 128), jnp.float32)
        after_decay = jnp.ones((1, 128), jnp.float32)
        for k in range(level_count):
            lbs, lbd, las, lad = level_refs[4 * k : 4 * k + 4]
            before_state = before_state + before_decay * lbs[...]
            before_decay = before_decay * lbd[...]
            after_state = after_state + after_decay * las[...]
            after_decay = after_decay * lad[...]
        for m in range(members):
            out_ref[m, 0:width, :] = bs_ref[m] + bd_ref[m] * before_state
            out_ref[m, width : 2 * width, :] = as_ref[m] + ad_ref[m] * after_state

    vmem = pl.BlockSpec(memory_space=pltpu.VMEM)
    return pl.pallas_call(
        kernel,
        out_shape=jax.ShapeDtypeStruct((members, 2 * width, 128), jnp.float32),
        in_specs=[vmem] * (4 + 4 * level_count),
        out_specs=vmem,
        interpret=INTERPRET,
    )


def both_prefixes(decay, fwd_state, bwd_state, levels):
    members = lax.axis_size("inner")
    width = fwd_state.shape[1]
    packed = jnp.concatenate(
        [fwd_state, bwd_state, jnp.broadcast_to(decay[:, None, None], decay.shape[:1] + (1,) + fwd_state.shape[2:])],
        axis=1,
    )
    mine = lax.all_to_all(packed, "inner", 0, 0, tiled=True)
    prefixes = inner_kernel(members, width)(mine)
    aggregate = (prefixes[6][None], prefixes[4][None], prefixes[5][None])
    level_parts = []
    for at, axis in enumerate(levels):
        parts, aggregate = level_exchange(aggregate, axis, at == len(levels) - 1)
        level_parts += list(parts)
    back = back_kernel(members, width, len(levels))(*prefixes[:4], *level_parts)
    shared = lax.all_to_all(back, "inner", 0, 0, tiled=True)
    return (shared[:, :width], shared[:, width:])


def head_scatter(total, axes):
    sizes = [lax.axis_size(axis) for axis in axes]
    blocks = total.reshape(tuple(sizes) + (total.shape[0] // math.prod(sizes),) + total.shape[1:])
    for place in range(len(axes) - 1, -1, -1):
        if sizes[place] == 2:
            upper = lax.axis_index(axes[place]) == 1
            low = lax.index_in_dim(blocks, 0, place, keepdims=False)
            high = lax.index_in_dim(blocks, 1, place, keepdims=False)
            got = lax.ppermute(jnp.where(upper, low, high), axes[place], [(0, 1), (1, 0)])
            blocks = jnp.where(upper, high, low) + got
        else:
            blocks = jnp.sum(lax.all_to_all(blocks, axes[place], place, place, tiled=True), axis=place)
    return blocks


def combine_forward(first_part, second_part):
    return (
        first_part[0] * second_part[0],
        second_part[1] + second_part[0][:, None, None] * first_part[1],
    )


def combine_backward(first_part, second_part):
    return (
        first_part[0] * second_part[0],
        second_part[1] + second_part[0][:, None, None] * first_part[1],
    )


def shards(head_input, step_size, log_decay, write_proj, read_proj, grad_out, levels, head_axes):
    highest = lax.Precision.HIGHEST
    head_count = step_size.shape[0]
    row_count = head_input.shape[0]
    head_width = head_input.shape[1] // head_count
    state_width = write_proj.shape[1]
    group_count = row_count // GROUP
    inputs = head_input.reshape(row_count, head_count, head_width).transpose(1, 2, 0)
    scaled = inputs * step_size[:, None, :]
    upstream = grad_out.reshape(row_count, head_count, head_width).transpose(1, 2, 0)
    row_ids = lax.broadcasted_iota(jnp.int32, (GROUP, GROUP), 0)
    col_ids = lax.broadcasted_iota(jnp.int32, (GROUP, GROUP), 1)
    lower_mask = row_ids >= col_ids
    lower_ones = lower_mask.astype(jnp.float32)
    blocks = []
    for position in range(group_count):
        offset = position * GROUP
        group_rates = log_decay[:, offset : offset + GROUP]
        scaled_part = scaled[:, :, offset : offset + GROUP]
        upstream_part = upstream[:, :, offset : offset + GROUP]
        write_part = write_proj[offset : offset + GROUP]
        read_part = read_proj[offset : offset + GROUP]
        cumulated = jnp.dot(group_rates, lower_ones.T, precision=highest)
        final_cum = cumulated[:, -1:]
        gap_logs = cumulated[:, :, None] - cumulated[:, None, :]
        decay_mat = jnp.where(
            lower_mask[None], jnp.exp(jnp.where(lower_mask[None], gap_logs, 0.0)), 0.0
        )
        inner_prod = jnp.dot(read_part, write_part.T, precision=highest)
        mixed_mat = inner_prod[None] * decay_mat
        out_near = jnp.einsum("hts,hps->hpt", mixed_mat, scaled_part, precision=highest)
        back_near = jnp.einsum("hst,hps->hpt", mixed_mat, upstream_part, precision=highest)
        pair_prods = jnp.einsum("hpt,hps->hts", upstream_part, scaled_part, precision=highest)
        weight_sum = jnp.sum(decay_mat * pair_prods, axis=0)
        read_near = jnp.dot(weight_sum, write_part, precision=highest)
        write_near = jnp.dot(weight_sum.T, read_part, precision=highest)
        into_factor = jnp.exp(cumulated)[:, None, :]
        outof_factor = jnp.exp(final_cum - cumulated)[:, None, :]
        whole_decay = jnp.exp(final_cum[:, 0])
        into_upstream = into_factor * upstream_part
        outof_scaled = outof_factor * scaled_part
        fwd_part = jnp.einsum("hps,sn->hpn", outof_scaled, write_part, precision=highest)
        bwd_part = jnp.einsum("hps,sn->hpn", into_upstream, read_part, precision=highest)
        blocks.append(
            (
                into_upstream,
                outof_scaled,
                write_part,
                read_part,
                into_factor,
                outof_factor,
                whole_decay,
                out_near,
                back_near,
                write_near,
                read_near,
                fwd_part,
                bwd_part,
            )
        )
    unit_decay = jnp.ones((head_count,), dtype=jnp.float32)
    zero_state = jnp.zeros((head_count, head_width, state_width), dtype=jnp.float32)
    fwd_decay, fwd_state = (unit_decay, zero_state)
    for entry in blocks:
        fwd_decay = fwd_decay * entry[6]
        fwd_state = entry[6][:, None, None] * fwd_state + entry[11]
    bwd_decay, bwd_state = (unit_decay, zero_state)
    for entry in reversed(blocks):
        bwd_decay = bwd_decay * entry[6]
        bwd_state = entry[12] + entry[6][:, None, None] * bwd_state
    state_in, grad_in = both_prefixes(fwd_decay, fwd_state, bwd_state, levels)
    entering = []
    current = state_in
    for entry in blocks:
        entering.append(current)
        current = entry[6][:, None, None] * current + entry[11]
    leaving = [None] * group_count
    current = grad_in
    for position in range(group_count - 1, -1, -1):
        leaving[position] = current
        current = blocks[position][12] + blocks[position][6][:, None, None] * current
    out_blocks, back_blocks, write_far, read_far = ([], [], [], [])
    for position in range(group_count):
        into_upstream, outof_scaled, write_part, read_part, into_factor, outof_factor = blocks[
            position
        ][:6]
        state_here = entering[position]
        state_after = leaving[position]
        out_blocks.append(
            blocks[position][7]
            + into_factor * jnp.einsum("tn,hpn->hpt", read_part, state_here, precision=highest)
        )
        back_blocks.append(
            blocks[position][8]
            + outof_factor * jnp.einsum("tn,hpn->hpt", write_part, state_after, precision=highest)
        )
        read_far.append(jnp.einsum("hpt,hpn->tn", into_upstream, state_here, precision=highest))
        write_far.append(jnp.einsum("hpt,hpn->tn", outof_scaled, state_after, precision=highest))
    result_rows = jnp.concatenate(out_blocks, axis=2)
    back_rows = jnp.concatenate(back_blocks, axis=2)
    write_carried = jnp.concatenate(write_far, axis=0)
    read_carried = jnp.concatenate(read_far, axis=0)
    write_total = jnp.concatenate([entry[9] for entry in blocks], axis=0) + write_carried
    read_total = jnp.concatenate([entry[10] for entry in blocks], axis=0) + read_carried
    both_grads = head_scatter(jnp.concatenate([write_total, read_total], axis=1), head_axes)
    write_grad, read_grad = (both_grads[:, :state_width], both_grads[:, state_width:])
    grad_input = (
        (step_size[:, None, :] * back_rows)
        .transpose(2, 0, 1)
        .reshape(row_count, head_count * head_width)
    )
    grad_step = jnp.sum(inputs * back_rows, axis=1)
    head_output = result_rows.transpose(2, 0, 1).reshape(row_count, head_count * head_width)
    return (head_output, grad_input, grad_step, write_grad, read_grad)


def solution(mesh):
    def run(*args):
        heads_here = args[1].shape[0] // mesh.shape["head"]
        ctx_count = mesh.shape["ctx"]
        inner = 1
        while inner < heads_here and inner < ctx_count and heads_here % (inner * 2) == 0:
            inner *= 2
        rest = ctx_count // inner
        factors = []
        while rest > 1:
            factor = 4 if rest % 4 == 0 else (2 if rest % 2 == 0 else rest)
            factors.append(factor)
            rest //= factor
        levels = tuple(f"level{k}" for k in range(len(factors)))
        head_count = mesh.shape["head"]
        pair = 2 if head_count % 2 == 0 else 1
        head_axes = ("head_outer", "head_inner")
        fine = Mesh(
            mesh.devices.reshape(tuple(reversed(factors)) + (inner, head_count // pair, pair)),
            tuple(reversed(levels)) + ("inner",) + head_axes,
        )
        head = head_axes
        ctx = tuple(reversed(levels)) + ("inner",)
        placed = (
            P(ctx, head),
            P(head, ctx),
            P(head, ctx),
            P(ctx, None),
            P(ctx, None),
            P(ctx, head),
        )
        return jax.shard_map(
            functools.partial(shards, levels=levels, head_axes=head_axes),
            mesh=fine,
            in_specs=placed,
            out_specs=(
                P(ctx, head),
                P(ctx, head),
                P(head, ctx),
                P(ctx + head, None),
                P(ctx + head, None),
            ),
            check_vma=False,
        )(*args)

    return run
```

```python
import functools
import math

import jax
import jax.numpy as jnp
from jax import lax
from jax.experimental import pallas as pl
from jax.experimental.pallas import tpu as pltpu
from jax.sharding import Mesh, PartitionSpec as P

GROUP = 128


def butterfly_rounds(shifts, size, here, span, before, after, final, axis):
    span_decay, span_fwd, span_bwd = span
    before_decay, before_state = before
    after_decay, after_state = after
    width = span_fwd.shape[1]
    extra = span_decay.shape[:1] + (1,) + span_fwd.shape[2:]
    for at, shift in enumerate(shifts):
        last = final and at == len(shifts) - 1
        upper = (here & shift) != 0
        pairs = [(j, j ^ shift) for j in range(size)]
        tail = jnp.broadcast_to(span_decay[:, None, None], extra)
        if last:
            packed = jnp.concatenate([jnp.where(upper, span_bwd, span_fwd), tail], axis=1)
        else:
            packed = jnp.concatenate([span_fwd, span_bwd, tail], axis=1)
        got = lax.ppermute(packed, axis, pairs)
        got_decay = got[:, -1, 0]
        if last:
            got_fwd = got_bwd = got[:, :width]
        else:
            got_fwd, got_bwd = (got[:, :width], got[:, width : 2 * width])
        scale = before_decay[:, None, None]
        before_state = jnp.where(upper, before_state + scale * got_fwd, before_state)
        before_decay = jnp.where(upper, before_decay * got_decay, before_decay)
        scale = after_decay[:, None, None]
        after_state = jnp.where(upper, after_state, after_state + scale * got_bwd)
        after_decay = jnp.where(upper, after_decay, after_decay * got_decay)
        if not last:
            mine = span_decay[:, None, None]
            theirs = got_decay[:, None, None]
            span_fwd = jnp.where(upper, span_fwd + mine * got_fwd, got_fwd + theirs * span_fwd)
            span_bwd = jnp.where(upper, got_bwd + theirs * span_bwd, span_bwd + mine * got_bwd)
            span_decay = span_decay * got_decay
    return ((span_decay, span_fwd, span_bwd), (before_decay, before_state), (after_decay, after_state))


INTERPRET = False


def level_kernel(count, width, last):
    rows = width + 1 if last else 2 * width + 1

    def kernel(here_ref, got_ref, *outs):
        here = here_ref[0]
        decays = [got_ref[s, rows - 1 : rows, :] for s in range(count)]
        fwds = [got_ref[s, 0:width, :] for s in range(count)]
        bwds = fwds if last else [got_ref[s, width : 2 * width, :] for s in range(count)]
        before_state = jnp.zeros((width, 128), jnp.float32)
        before_decay = jnp.ones((1, 128), jnp.float32)
        for s in range(count):
            take = s < here
            factor = jnp.where(take, decays[s], 1.0)
            before_state = factor * before_state + jnp.where(take, fwds[s], 0.0)
            before_decay = before_decay * factor
        after_state = jnp.zeros((width, 128), jnp.float32)
        after_decay = jnp.ones((1, 128), jnp.float32)
        for s in range(count - 1, -1, -1):
            take = s > here
            factor = jnp.where(take, decays[s], 1.0)
            after_state = jnp.where(take, bwds[s], 0.0) + factor * after_state
            after_decay = after_decay * factor
        outs[0][...] = before_state
        outs[1][...] = before_decay
        outs[2][...] = after_state
        outs[3][...] = after_decay
        if not last:
            span_fwd = jnp.zeros((width, 128), jnp.float32)
            span_decay = jnp.ones((1, 128), jnp.float32)
            for s in range(count):
                span_fwd = decays[s] * span_fwd + fwds[s]
                span_decay = span_decay * decays[s]
            span_bwd = jnp.zeros((width, 128), jnp.float32)
            for s in range(count - 1, -1, -1):
                span_bwd = bwds[s] + decays[s] * span_bwd
            outs[4][...] = span_fwd
            outs[5][...] = span_bwd
            outs[6][...] = span_decay

    state = jax.ShapeDtypeStruct((width, 128), jnp.float32)
    row = jax.ShapeDtypeStruct((1, 128), jnp.float32)
    shapes = (state, row, state, row) + (() if last else (state, state, row))
    vmem = pl.BlockSpec(memory_space=pltpu.VMEM)
    return pl.pallas_call(
        kernel,
        out_shape=shapes,
        in_specs=[pl.BlockSpec(memory_space=pltpu.SMEM), vmem],
        out_specs=tuple(vmem for _ in shapes),
        interpret=INTERPRET,
    )


def level_exchange(aggregate, axis, last, ready=None):
    count, here = (lax.axis_size(axis), lax.axis_index(axis))
    tail, fwd, bwd = aggregate
    width = fwd.shape[1]
    if last:
        sent = jnp.stack(
            [jnp.concatenate([jnp.where(m < here, bwd, fwd), tail], axis=1) for m in range(count)]
        )
    elif ready is not None:
        sent = ready
    else:
        packed = jnp.concatenate([fwd, bwd, tail], axis=1)
        sent = jnp.broadcast_to(packed[None], (count,) + packed.shape)
    got = lax.all_to_all(sent, axis, 0, 0)
    got = got.reshape((count,) + got.shape[2:])
    outs = level_kernel(count, width, last)(jnp.reshape(here, (1,)).astype(jnp.int32), got)
    if last:
        return (outs, None)
    return (outs[:4], (outs[6][None], outs[4][None], outs[5][None]))


def inner_kernel(members, width, copies):
    def kernel(mine_ref, bs_ref, bd_ref, as_ref, ad_ref, sf_ref, sb_ref, sd_ref, packed_ref):
        rows = 2 * width + 1
        decays = [mine_ref[m, rows - 1 : rows, :] for m in range(members)]
        run_state = jnp.zeros((width, 128), jnp.float32)
        run_decay = jnp.ones((1, 128), jnp.float32)
        for m in range(members):
            bs_ref[m] = run_state
            bd_ref[m] = run_decay
            run_state = decays[m] * run_state + mine_ref[m, 0:width, :]
            run_decay = run_decay * decays[m]
        sf_ref[...] = run_state
        sd_ref[...] = run_decay
        run_state = jnp.zeros((width, 128), jnp.float32)
        run_decay = jnp.ones((1, 128), jnp.float32)
        for m in range(members - 1, -1, -1):
            as_ref[m] = run_state
            ad_ref[m] = run_decay
            run_state = mine_ref[m, width : 2 * width, :] + decays[m] * run_state
            run_decay = run_decay * decays[m]
        sb_ref[...] = run_state
        for c in range(copies):
            packed_ref[c, 0, 0:width, :] = sf_ref[...]
            packed_ref[c, 0, width : 2 * width, :] = run_state
            packed_ref[c, 0, 2 * width : 2 * width + 1, :] = sd_ref[...]

    many = jax.ShapeDtypeStruct((members, width, 128), jnp.float32)
    many_rows = jax.ShapeDtypeStruct((members, 1, 128), jnp.float32)
    state = jax.ShapeDtypeStruct((width, 128), jnp.float32)
    row = jax.ShapeDtypeStruct((1, 128), jnp.float32)
    packed = jax.ShapeDtypeStruct((copies, 1, 2 * width + 1, 128), jnp.float32)
    shapes = (many, many_rows, many, many_rows, state, state, row, packed)
    vmem = pl.BlockSpec(memory_space=pltpu.VMEM)
    return pl.pallas_call(
        kernel, out_shape=shapes, in_specs=[vmem], out_specs=tuple(vmem for _ in shapes), interpret=INTERPRET
    )


def back_kernel(members, width, level_count):
    def kernel(*refs):
        bs_ref, bd_ref, as_ref, ad_ref = refs[:4]
        level_refs = refs[4 : 4 + 4 * level_count]
        out_ref = refs[-1]
        before_state = jnp.zeros((width, 128), jnp.float32)
        before_decay = jnp.ones((1, 128), jnp.float32)
        after_state = jnp.zeros((width, 128), jnp.float32)
        after_decay = jnp.ones((1, 128), jnp.float32)
        for k in range(level_count):
            lbs, lbd, las, lad = level_refs[4 * k : 4 * k + 4]
            before_state = before_state + before_decay * lbs[...]
            before_decay = before_decay * lbd[...]
            after_state = after_state + after_decay * las[...]
            after_decay = after_decay * lad[...]
        for m in range(members):
            out_ref[m, 0:width, :] = bs_ref[m] + bd_ref[m] * before_state
            out_ref[m, width : 2 * width, :] = as_ref[m] + ad_ref[m] * after_state

    vmem = pl.BlockSpec(memory_space=pltpu.VMEM)
    return pl.pallas_call(
        kernel,
        out_shape=jax.ShapeDtypeStruct((members, 2 * width, 128), jnp.float32),
        in_specs=[vmem] * (4 + 4 * level_count),
        out_specs=vmem,
        interpret=INTERPRET,
    )


def both_prefixes(decay, fwd_state, bwd_state, levels):
    members = lax.axis_size("inner")
    width = fwd_state.shape[1]
    packed = jnp.concatenate(
        [fwd_state, bwd_state, jnp.broadcast_to(decay[:, None, None], decay.shape[:1] + (1,) + fwd_state.shape[2:])],
        axis=1,
    )
    mine = lax.all_to_all(packed, "inner", 0, 0, tiled=True)
    prefixes = inner_kernel(members, width, lax.axis_size(levels[0]))(mine)
    aggregate = (prefixes[6][None], prefixes[4][None], prefixes[5][None])
    level_parts = []
    for at, axis in enumerate(levels):
        ready = prefixes[7] if at == 0 and len(levels) > 1 else None
        parts, aggregate = level_exchange(aggregate, axis, at == len(levels) - 1, ready)
        level_parts += list(parts)
    back = back_kernel(members, width, len(levels))(*prefixes[:4], *level_parts)
    shared = lax.all_to_all(back, "inner", 0, 0, tiled=True)
    return (shared[:, :width], shared[:, width:])


def head_scatter(total, axes):
    sizes = [lax.axis_size(axis) for axis in axes]
    blocks = total.reshape(tuple(sizes) + (total.shape[0] // math.prod(sizes),) + total.shape[1:])
    for place in range(len(axes) - 1, -1, -1):
        blocks = jnp.sum(lax.all_to_all(blocks, axes[place], place, place, tiled=True), axis=place)
    return blocks


def combine_forward(first_part, second_part):
    return (
        first_part[0] * second_part[0],
        second_part[1] + second_part[0][:, None, None] * first_part[1],
    )


def combine_backward(first_part, second_part):
    return (
        first_part[0] * second_part[0],
        second_part[1] + second_part[0][:, None, None] * first_part[1],
    )


def shards(head_input, step_size, log_decay, write_proj, read_proj, grad_out, levels, head_axes):
    highest = lax.Precision.HIGHEST
    head_count = step_size.shape[0]
    row_count = head_input.shape[0]
    head_width = head_input.shape[1] // head_count
    state_width = write_proj.shape[1]
    group_count = row_count // GROUP
    inputs = head_input.reshape(row_count, head_count, head_width).transpose(1, 2, 0)
    scaled = inputs * step_size[:, None, :]
    upstream = grad_out.reshape(row_count, head_count, head_width).transpose(1, 2, 0)
    row_ids = lax.broadcasted_iota(jnp.int32, (GROUP, GROUP), 0)
    col_ids = lax.broadcasted_iota(jnp.int32, (GROUP, GROUP), 1)
    lower_mask = row_ids >= col_ids
    lower_ones = lower_mask.astype(jnp.float32)
    blocks = []
    for position in range(group_count):
        offset = position * GROUP
        group_rates = log_decay[:, offset : offset + GROUP]
        scaled_part = scaled[:, :, offset : offset + GROUP]
        upstream_part = upstream[:, :, offset : offset + GROUP]
        write_part = write_proj[offset : offset + GROUP]
        read_part = read_proj[offset : offset + GROUP]
        cumulated = jnp.dot(group_rates, lower_ones.T, precision=highest)
        final_cum = cumulated[:, -1:]
        gap_logs = cumulated[:, :, None] - cumulated[:, None, :]
        decay_mat = jnp.where(
            lower_mask[None], jnp.exp(jnp.where(lower_mask[None], gap_logs, 0.0)), 0.0
        )
        inner_prod = jnp.dot(read_part, write_part.T, precision=highest)
        mixed_mat = inner_prod[None] * decay_mat
        out_near = jnp.einsum("hts,hps->hpt", mixed_mat, scaled_part, precision=highest)
        back_near = jnp.einsum("hst,hps->hpt", mixed_mat, upstream_part, precision=highest)
        pair_prods = jnp.einsum("hpt,hps->hts", upstream_part, scaled_part, precision=highest)
        weight_sum = jnp.sum(decay_mat * pair_prods, axis=0)
        read_near = jnp.dot(weight_sum, write_part, precision=highest)
        write_near = jnp.dot(weight_sum.T, read_part, precision=highest)
        into_factor = jnp.exp(cumulated)[:, None, :]
        outof_factor = jnp.exp(final_cum - cumulated)[:, None, :]
        whole_decay = jnp.exp(final_cum[:, 0])
        into_upstream = into_factor * upstream_part
        outof_scaled = outof_factor * scaled_part
        fwd_part = jnp.einsum("hps,sn->hpn", outof_scaled, write_part, precision=highest)
        bwd_part = jnp.einsum("hps,sn->hpn", into_upstream, read_part, precision=highest)
        blocks.append(
            (
                into_upstream,
                outof_scaled,
                write_part,
                read_part,
                into_factor,
                outof_factor,
                whole_decay,
                out_near,
                back_near,
                write_near,
                read_near,
                fwd_part,
                bwd_part,
            )
        )
    unit_decay = jnp.ones((head_count,), dtype=jnp.float32)
    zero_state = jnp.zeros((head_count, head_width, state_width), dtype=jnp.float32)
    fwd_decay, fwd_state = (unit_decay, zero_state)
    for entry in blocks:
        fwd_decay = fwd_decay * entry[6]
        fwd_state = entry[6][:, None, None] * fwd_state + entry[11]
    bwd_decay, bwd_state = (unit_decay, zero_state)
    for entry in reversed(blocks):
        bwd_decay = bwd_decay * entry[6]
        bwd_state = entry[12] + entry[6][:, None, None] * bwd_state
    state_in, grad_in = both_prefixes(fwd_decay, fwd_state, bwd_state, levels)
    entering = []
    current = state_in
    for entry in blocks:
        entering.append(current)
        current = entry[6][:, None, None] * current + entry[11]
    leaving = [None] * group_count
    current = grad_in
    for position in range(group_count - 1, -1, -1):
        leaving[position] = current
        current = blocks[position][12] + blocks[position][6][:, None, None] * current
    out_blocks, back_blocks, write_far, read_far = ([], [], [], [])
    for position in range(group_count):
        into_upstream, outof_scaled, write_part, read_part, into_factor, outof_factor = blocks[
            position
        ][:6]
        state_here = entering[position]
        state_after = leaving[position]
        out_blocks.append(
            blocks[position][7]
            + into_factor * jnp.einsum("tn,hpn->hpt", read_part, state_here, precision=highest)
        )
        back_blocks.append(
            blocks[position][8]
            + outof_factor * jnp.einsum("tn,hpn->hpt", write_part, state_after, precision=highest)
        )
        read_far.append(jnp.einsum("hpt,hpn->tn", into_upstream, state_here, precision=highest))
        write_far.append(jnp.einsum("hpt,hpn->tn", outof_scaled, state_after, precision=highest))
    result_rows = jnp.concatenate(out_blocks, axis=2)
    back_rows = jnp.concatenate(back_blocks, axis=2)
    write_carried = jnp.concatenate(write_far, axis=0)
    read_carried = jnp.concatenate(read_far, axis=0)
    write_total = jnp.concatenate([entry[9] for entry in blocks], axis=0) + write_carried
    read_total = jnp.concatenate([entry[10] for entry in blocks], axis=0) + read_carried
    both_grads = head_scatter(jnp.concatenate([write_total, read_total], axis=1), head_axes)
    write_grad, read_grad = (both_grads[:, :state_width], both_grads[:, state_width:])
    grad_input = (
        (step_size[:, None, :] * back_rows)
        .transpose(2, 0, 1)
        .reshape(row_count, head_count * head_width)
    )
    grad_step = jnp.sum(inputs * back_rows, axis=1)
    head_output = result_rows.transpose(2, 0, 1).reshape(row_count, head_count * head_width)
    return (head_output, grad_input, grad_step, write_grad, read_grad)


def solution(mesh):
    def run(*args):
        heads_here = args[1].shape[0] // mesh.shape["head"]
        ctx_count = mesh.shape["ctx"]
        inner = 1
        while inner < heads_here and inner < ctx_count and heads_here % (inner * 2) == 0:
            inner *= 2
        rest = ctx_count // inner
        factors = []
        while rest > 1:
            factor = 4 if rest % 4 == 0 else (2 if rest % 2 == 0 else rest)
            factors.append(factor)
            rest //= factor
        levels = tuple(f"level{k}" for k in range(len(factors)))
        head_count = mesh.shape["head"]
        pair = 2 if head_count % 2 == 0 else 1
        head_axes = ("head_outer", "head_inner")
        fine = Mesh(
            mesh.devices.reshape(tuple(reversed(factors)) + (inner, head_count // pair, pair)),
            tuple(reversed(levels)) + ("inner",) + head_axes,
        )
        head = head_axes
        ctx = tuple(reversed(levels)) + ("inner",)
        placed = (
            P(ctx, head),
            P(head, ctx),
            P(head, ctx),
            P(ctx, None),
            P(ctx, None),
            P(ctx, head),
        )
        return jax.shard_map(
            functools.partial(shards, levels=levels, head_axes=head_axes),
            mesh=fine,
            in_specs=placed,
            out_specs=(
                P(ctx, head),
                P(ctx, head),
                P(head, ctx),
                P(ctx + head, None),
                P(ctx + head, None),
            ),
            check_vma=False,
        )(*args)

    return run
```

```python
import functools
import math

import jax
import jax.numpy as jnp
from jax import lax
from jax.experimental import pallas as pl
from jax.experimental.pallas import tpu as pltpu
from jax.sharding import Mesh, PartitionSpec as P

GROUP = 128


def butterfly_rounds(shifts, size, here, span, before, after, final, axis):
    span_decay, span_fwd, span_bwd = span
    before_decay, before_state = before
    after_decay, after_state = after
    width = span_fwd.shape[1]
    extra = span_decay.shape[:1] + (1,) + span_fwd.shape[2:]
    for at, shift in enumerate(shifts):
        last = final and at == len(shifts) - 1
        upper = (here & shift) != 0
        pairs = [(j, j ^ shift) for j in range(size)]
        tail = jnp.broadcast_to(span_decay[:, None, None], extra)
        if last:
            packed = jnp.concatenate([jnp.where(upper, span_bwd, span_fwd), tail], axis=1)
        else:
            packed = jnp.concatenate([span_fwd, span_bwd, tail], axis=1)
        got = lax.ppermute(packed, axis, pairs)
        got_decay = got[:, -1, 0]
        if last:
            got_fwd = got_bwd = got[:, :width]
        else:
            got_fwd, got_bwd = (got[:, :width], got[:, width : 2 * width])
        scale = before_decay[:, None, None]
        before_state = jnp.where(upper, before_state + scale * got_fwd, before_state)
        before_decay = jnp.where(upper, before_decay * got_decay, before_decay)
        scale = after_decay[:, None, None]
        after_state = jnp.where(upper, after_state, after_state + scale * got_bwd)
        after_decay = jnp.where(upper, after_decay, after_decay * got_decay)
        if not last:
            mine = span_decay[:, None, None]
            theirs = got_decay[:, None, None]
            span_fwd = jnp.where(upper, span_fwd + mine * got_fwd, got_fwd + theirs * span_fwd)
            span_bwd = jnp.where(upper, got_bwd + theirs * span_bwd, span_bwd + mine * got_bwd)
            span_decay = span_decay * got_decay
    return ((span_decay, span_fwd, span_bwd), (before_decay, before_state), (after_decay, after_state))


INTERPRET = False


def level_kernel(count, width, last, next_count=0):
    rows = width + 1 if last else 2 * width + 1

    def kernel(here_ref, got_ref, *outs):
        here = here_ref[0]
        decays = [got_ref[s, rows - 1 : rows, :] for s in range(count)]
        fwds = [got_ref[s, 0:width, :] for s in range(count)]
        bwds = fwds if last else [got_ref[s, width : 2 * width, :] for s in range(count)]
        before_state = jnp.zeros((width, 128), jnp.float32)
        before_decay = jnp.ones((1, 128), jnp.float32)
        for s in range(count):
            take = s < here
            factor = jnp.where(take, decays[s], 1.0)
            before_state = factor * before_state + jnp.where(take, fwds[s], 0.0)
            before_decay = before_decay * factor
        after_state = jnp.zeros((width, 128), jnp.float32)
        after_decay = jnp.ones((1, 128), jnp.float32)
        for s in range(count - 1, -1, -1):
            take = s > here
            factor = jnp.where(take, decays[s], 1.0)
            after_state = jnp.where(take, bwds[s], 0.0) + factor * after_state
            after_decay = after_decay * factor
        outs[0][...] = before_state
        outs[1][...] = before_decay
        outs[2][...] = after_state
        outs[3][...] = after_decay
        if not last:
            span_fwd = jnp.zeros((width, 128), jnp.float32)
            span_decay = jnp.ones((1, 128), jnp.float32)
            for s in range(count):
                span_fwd = decays[s] * span_fwd + fwds[s]
                span_decay = span_decay * decays[s]
            span_bwd = jnp.zeros((width, 128), jnp.float32)
            for s in range(count - 1, -1, -1):
                span_bwd = bwds[s] + decays[s] * span_bwd
            outs[4][...] = span_fwd
            outs[5][...] = span_bwd
            outs[6][...] = span_decay
            if next_count:
                following = here_ref[1]
                for m in range(next_count):
                    outs[7][m, 0, 0:width, :] = jnp.where(m < following, span_bwd, span_fwd)
                    outs[7][m, 0, width : width + 1, :] = span_decay

    state = jax.ShapeDtypeStruct((width, 128), jnp.float32)
    row = jax.ShapeDtypeStruct((1, 128), jnp.float32)
    shapes = (state, row, state, row) + (() if last else (state, state, row))
    if next_count:
        shapes = shapes + (jax.ShapeDtypeStruct((next_count, 1, width + 1, 128), jnp.float32),)
    vmem = pl.BlockSpec(memory_space=pltpu.VMEM)
    return pl.pallas_call(
        kernel,
        out_shape=shapes,
        in_specs=[pl.BlockSpec(memory_space=pltpu.SMEM), vmem],
        out_specs=tuple(vmem for _ in shapes),
        interpret=INTERPRET,
    )


def level_exchange(aggregate, axis, last, ready=None, next_axis=None):
    count, here = (lax.axis_size(axis), lax.axis_index(axis))
    width = aggregate[1].shape[1] if isinstance(aggregate, tuple) else aggregate.shape[2] - 1
    if isinstance(aggregate, tuple):
        tail, fwd, bwd = aggregate
    if last and not isinstance(aggregate, tuple):
        sent = aggregate
    elif last:
        sent = jnp.stack(
            [jnp.concatenate([jnp.where(m < here, bwd, fwd), tail], axis=1) for m in range(count)]
        )
    elif ready is not None:
        sent = ready
    else:
        packed = jnp.concatenate([fwd, bwd, tail], axis=1)
        sent = jnp.broadcast_to(packed[None], (count,) + packed.shape)
    got = lax.all_to_all(sent, axis, 0, 0)
    got = got.reshape((count,) + got.shape[2:])
    next_count = lax.axis_size(next_axis) if next_axis is not None else 0
    following = lax.axis_index(next_axis) if next_axis is not None else 0
    indices = jnp.stack([jnp.asarray(here, jnp.int32), jnp.asarray(following, jnp.int32)])
    outs = level_kernel(count, width, last, next_count)(indices, got)
    if last:
        return (outs, None)
    if next_count:
        return (outs[:4], outs[7])
    return (outs[:4], (outs[6][None], outs[4][None], outs[5][None]))


def inner_kernel(members, width, copies):
    def kernel(mine_ref, bs_ref, bd_ref, as_ref, ad_ref, sf_ref, sb_ref, sd_ref, packed_ref):
        rows = 2 * width + 1
        decays = [mine_ref[m, rows - 1 : rows, :] for m in range(members)]
        run_state = jnp.zeros((width, 128), jnp.float32)
        run_decay = jnp.ones((1, 128), jnp.float32)
        for m in range(members):
            bs_ref[m] = run_state
            bd_ref[m] = run_decay
            run_state = decays[m] * run_state + mine_ref[m, 0:width, :]
            run_decay = run_decay * decays[m]
        sf_ref[...] = run_state
        sd_ref[...] = run_decay
        run_state = jnp.zeros((width, 128), jnp.float32)
        run_decay = jnp.ones((1, 128), jnp.float32)
        for m in range(members - 1, -1, -1):
            as_ref[m] = run_state
            ad_ref[m] = run_decay
            run_state = mine_ref[m, width : 2 * width, :] + decays[m] * run_state
            run_decay = run_decay * decays[m]
        sb_ref[...] = run_state
        for c in range(copies):
            packed_ref[c, 0, 0:width, :] = sf_ref[...]
            packed_ref[c, 0, width : 2 * width, :] = run_state
            packed_ref[c, 0, 2 * width : 2 * width + 1, :] = sd_ref[...]

    many = jax.ShapeDtypeStruct((members, width, 128), jnp.float32)
    many_rows = jax.ShapeDtypeStruct((members, 1, 128), jnp.float32)
    state = jax.ShapeDtypeStruct((width, 128), jnp.float32)
    row = jax.ShapeDtypeStruct((1, 128), jnp.float32)
    packed = jax.ShapeDtypeStruct((copies, 1, 2 * width + 1, 128), jnp.float32)
    shapes = (many, many_rows, many, many_rows, state, state, row, packed)
    vmem = pl.BlockSpec(memory_space=pltpu.VMEM)
    return pl.pallas_call(
        kernel, out_shape=shapes, in_specs=[vmem], out_specs=tuple(vmem for _ in shapes), interpret=INTERPRET
    )


def back_kernel(members, width, level_count):
    def kernel(*refs):
        bs_ref, bd_ref, as_ref, ad_ref = refs[:4]
        level_refs = refs[4 : 4 + 4 * level_count]
        out_ref = refs[-1]
        before_state = jnp.zeros((width, 128), jnp.float32)
        before_decay = jnp.ones((1, 128), jnp.float32)
        after_state = jnp.zeros((width, 128), jnp.float32)
        after_decay = jnp.ones((1, 128), jnp.float32)
        for k in range(level_count):
            lbs, lbd, las, lad = level_refs[4 * k : 4 * k + 4]
            before_state = before_state + before_decay * lbs[...]
            before_decay = before_decay * lbd[...]
            after_state = after_state + after_decay * las[...]
            after_decay = after_decay * lad[...]
        for m in range(members):
            out_ref[m, 0:width, :] = bs_ref[m] + bd_ref[m] * before_state
            out_ref[m, width : 2 * width, :] = as_ref[m] + ad_ref[m] * after_state

    vmem = pl.BlockSpec(memory_space=pltpu.VMEM)
    return pl.pallas_call(
        kernel,
        out_shape=jax.ShapeDtypeStruct((members, 2 * width, 128), jnp.float32),
        in_specs=[vmem] * (4 + 4 * level_count),
        out_specs=vmem,
        interpret=INTERPRET,
    )


def both_prefixes(decay, fwd_state, bwd_state, levels):
    members = lax.axis_size("inner")
    width = fwd_state.shape[1]
    packed = jnp.concatenate(
        [fwd_state, bwd_state, jnp.broadcast_to(decay[:, None, None], decay.shape[:1] + (1,) + fwd_state.shape[2:])],
        axis=1,
    )
    mine = lax.all_to_all(packed, "inner", 0, 0, tiled=True)
    prefixes = inner_kernel(members, width, lax.axis_size(levels[0]))(mine)
    aggregate = (prefixes[6][None], prefixes[4][None], prefixes[5][None])
    level_parts = []
    for at, axis in enumerate(levels):
        ready = prefixes[7] if at == 0 and len(levels) > 1 else None
        following = levels[at + 1] if at + 2 == len(levels) else None
        parts, aggregate = level_exchange(aggregate, axis, at == len(levels) - 1, ready, following)
        level_parts += list(parts)
    back = back_kernel(members, width, len(levels))(*prefixes[:4], *level_parts)
    shared = lax.all_to_all(back, "inner", 0, 0, tiled=True)
    return (shared[:, :width], shared[:, width:])


def head_scatter(total, axes):
    sizes = [lax.axis_size(axis) for axis in axes]
    blocks = total.reshape(tuple(sizes) + (total.shape[0] // math.prod(sizes),) + total.shape[1:])
    for place in range(len(axes) - 1, -1, -1):
        blocks = jnp.sum(lax.all_to_all(blocks, axes[place], place, place, tiled=True), axis=place)
    return blocks


def combine_forward(first_part, second_part):
    return (
        first_part[0] * second_part[0],
        second_part[1] + second_part[0][:, None, None] * first_part[1],
    )


def combine_backward(first_part, second_part):
    return (
        first_part[0] * second_part[0],
        second_part[1] + second_part[0][:, None, None] * first_part[1],
    )


def shards(head_input, step_size, log_decay, write_proj, read_proj, grad_out, levels, head_axes):
    highest = lax.Precision.HIGHEST
    head_count = step_size.shape[0]
    row_count = head_input.shape[0]
    head_width = head_input.shape[1] // head_count
    state_width = write_proj.shape[1]
    group_count = row_count // GROUP
    inputs = head_input.reshape(row_count, head_count, head_width).transpose(1, 2, 0)
    scaled = inputs * step_size[:, None, :]
    upstream = grad_out.reshape(row_count, head_count, head_width).transpose(1, 2, 0)
    row_ids = lax.broadcasted_iota(jnp.int32, (GROUP, GROUP), 0)
    col_ids = lax.broadcasted_iota(jnp.int32, (GROUP, GROUP), 1)
    lower_mask = row_ids >= col_ids
    lower_ones = lower_mask.astype(jnp.float32)
    blocks = []
    for position in range(group_count):
        offset = position * GROUP
        group_rates = log_decay[:, offset : offset + GROUP]
        scaled_part = scaled[:, :, offset : offset + GROUP]
        upstream_part = upstream[:, :, offset : offset + GROUP]
        write_part = write_proj[offset : offset + GROUP]
        read_part = read_proj[offset : offset + GROUP]
        cumulated = jnp.dot(group_rates, lower_ones.T, precision=highest)
        final_cum = cumulated[:, -1:]
        gap_logs = cumulated[:, :, None] - cumulated[:, None, :]
        decay_mat = jnp.where(
            lower_mask[None], jnp.exp(jnp.where(lower_mask[None], gap_logs, 0.0)), 0.0
        )
        inner_prod = jnp.dot(read_part, write_part.T, precision=highest)
        mixed_mat = inner_prod[None] * decay_mat
        out_near = jnp.einsum("hts,hps->hpt", mixed_mat, scaled_part, precision=highest)
        back_near = jnp.einsum("hst,hps->hpt", mixed_mat, upstream_part, precision=highest)
        pair_prods = jnp.einsum("hpt,hps->hts", upstream_part, scaled_part, precision=highest)
        weight_sum = jnp.sum(decay_mat * pair_prods, axis=0)
        read_near = jnp.dot(weight_sum, write_part, precision=highest)
        write_near = jnp.dot(weight_sum.T, read_part, precision=highest)
        into_factor = jnp.exp(cumulated)[:, None, :]
        outof_factor = jnp.exp(final_cum - cumulated)[:, None, :]
        whole_decay = jnp.exp(final_cum[:, 0])
        into_upstream = into_factor * upstream_part
        outof_scaled = outof_factor * scaled_part
        fwd_part = jnp.einsum("hps,sn->hpn", outof_scaled, write_part, precision=highest)
        bwd_part = jnp.einsum("hps,sn->hpn", into_upstream, read_part, precision=highest)
        blocks.append(
            (
                into_upstream,
                outof_scaled,
                write_part,
                read_part,
                into_factor,
                outof_factor,
                whole_decay,
                out_near,
                back_near,
                write_near,
                read_near,
                fwd_part,
                bwd_part,
            )
        )
    unit_decay = jnp.ones((head_count,), dtype=jnp.float32)
    zero_state = jnp.zeros((head_count, head_width, state_width), dtype=jnp.float32)
    fwd_decay, fwd_state = (unit_decay, zero_state)
    for entry in blocks:
        fwd_decay = fwd_decay * entry[6]
        fwd_state = entry[6][:, None, None] * fwd_state + entry[11]
    bwd_decay, bwd_state = (unit_decay, zero_state)
    for entry in reversed(blocks):
        bwd_decay = bwd_decay * entry[6]
        bwd_state = entry[12] + entry[6][:, None, None] * bwd_state
    state_in, grad_in = both_prefixes(fwd_decay, fwd_state, bwd_state, levels)
    entering = []
    current = state_in
    for entry in blocks:
        entering.append(current)
        current = entry[6][:, None, None] * current + entry[11]
    leaving = [None] * group_count
    current = grad_in
    for position in range(group_count - 1, -1, -1):
        leaving[position] = current
        current = blocks[position][12] + blocks[position][6][:, None, None] * current
    out_blocks, back_blocks, write_far, read_far = ([], [], [], [])
    for position in range(group_count):
        into_upstream, outof_scaled, write_part, read_part, into_factor, outof_factor = blocks[
            position
        ][:6]
        state_here = entering[position]
        state_after = leaving[position]
        out_blocks.append(
            blocks[position][7]
            + into_factor * jnp.einsum("tn,hpn->hpt", read_part, state_here, precision=highest)
        )
        back_blocks.append(
            blocks[position][8]
            + outof_factor * jnp.einsum("tn,hpn->hpt", write_part, state_after, precision=highest)
        )
        read_far.append(jnp.einsum("hpt,hpn->tn", into_upstream, state_here, precision=highest))
        write_far.append(jnp.einsum("hpt,hpn->tn", outof_scaled, state_after, precision=highest))
    result_rows = jnp.concatenate(out_blocks, axis=2)
    back_rows = jnp.concatenate(back_blocks, axis=2)
    write_carried = jnp.concatenate(write_far, axis=0)
    read_carried = jnp.concatenate(read_far, axis=0)
    write_total = jnp.concatenate([entry[9] for entry in blocks], axis=0) + write_carried
    read_total = jnp.concatenate([entry[10] for entry in blocks], axis=0) + read_carried
    both_grads = head_scatter(jnp.concatenate([write_total, read_total], axis=1), head_axes)
    write_grad, read_grad = (both_grads[:, :state_width], both_grads[:, state_width:])
    grad_input = (
        (step_size[:, None, :] * back_rows)
        .transpose(2, 0, 1)
        .reshape(row_count, head_count * head_width)
    )
    grad_step = jnp.sum(inputs * back_rows, axis=1)
    head_output = result_rows.transpose(2, 0, 1).reshape(row_count, head_count * head_width)
    return (head_output, grad_input, grad_step, write_grad, read_grad)


def solution(mesh):
    def run(*args):
        heads_here = args[1].shape[0] // mesh.shape["head"]
        ctx_count = mesh.shape["ctx"]
        inner = 1
        while inner < heads_here and inner < ctx_count and heads_here % (inner * 2) == 0:
            inner *= 2
        rest = ctx_count // inner
        factors = []
        while rest > 1:
            factor = 4 if rest % 4 == 0 else (2 if rest % 2 == 0 else rest)
            factors.append(factor)
            rest //= factor
        levels = tuple(f"level{k}" for k in range(len(factors)))
        head_count = mesh.shape["head"]
        pair = 2 if head_count % 2 == 0 else 1
        head_axes = ("head_outer", "head_inner")
        fine = Mesh(
            mesh.devices.reshape(tuple(reversed(factors)) + (inner, head_count // pair, pair)),
            tuple(reversed(levels)) + ("inner",) + head_axes,
        )
        head = head_axes
        ctx = tuple(reversed(levels)) + ("inner",)
        placed = (
            P(ctx, head),
            P(head, ctx),
            P(head, ctx),
            P(ctx, None),
            P(ctx, None),
            P(ctx, head),
        )
        return jax.shard_map(
            functools.partial(shards, levels=levels, head_axes=head_axes),
            mesh=fine,
            in_specs=placed,
            out_specs=(
                P(ctx, head),
                P(ctx, head),
                P(head, ctx),
                P(ctx + head, None),
                P(ctx + head, None),
            ),
            check_vma=False,
        )(*args)

    return run
```
